32 devices in a mesh: group: 2 (over x), region: 16 (over z, y, core).
Axes of the slice: x: 2, y: 2, z: 4, core: 2. Of those that a mesh axis runs over, the one named last changes fastest.
Arguments:
- first_map: bfloat16 [64, 512, 256], P('region', 'group'), parts along dimension 1, may hold values from -6 to 6
- second_map: bfloat16 [64, 512, 256], P('region', 'group'), parts along dimension 1, may hold values from -6 to 6
- flow_target: float32 [2, 64, 512], P(None, 'region', 'group'), parts along dimension 2, may hold values from -48 to 48
- valid_tiles: int32 [4, 32], P(None, 'group'), parts along dimension 1, may hold values 0 or 1
- conv_weight: bfloat16 [9, 81, 256], replicated, may hold values from -0.21875 to 0.21875
- conv_bias: float32 [256], replicated, may hold values from -3 to 3
- head_weight: bfloat16 [2, 256], replicated, may hold values from -4 to 4
Outputs:
- first_grad: bfloat16 [64, 512, 256], P('region', 'group'), parts along dimension 1
- second_grad: bfloat16 [64, 512, 256], P('region', 'group'), parts along dimension 1
- conv_grad: float32 [18, 81, 256], P('group', None, 'region'), parts along dimension 0
- bias_grad: float32 [512], P(('group', 'region')), parts along dimension 0
- head_grad: float32 [4, 256], P('group', 'region'), parts along dimension 0
The draws below stay inside these ranges and needn't reach their ends.
There are 2 independent parts, one for each index of `group`. The reference program is written for one: setup_inputs(seed, part) draws one part's arguments, and reference() takes and returns one part's arrays. A program takes and returns all parts, laid end to end along the dimension named above; an argument that names none is the same for every part. Nothing has to cross between parts.
All inputs are finite; a program needn't handle non-finite values.
Results may differ from the reference program's by a relative error of at most 0.007.
Values may be sent and summed in bfloat16 or wider, within the bound.
No kernel may reach another device: no remote copies, remote signals or barrier semaphores. Data moves between devices by JAX's collectives and lax.ppermute only.
A program may use at most 64 MiB of HBM per device.

```python
import math
import jax
import jax.numpy as jnp
from jax import lax

C = 256
HID = 256
RADIUS = 4
TILE = 16
COLS = 256
K = 81
NROWS = 64


def draw_head_weight(key, part):
    rising = jnp.arange(HID, dtype=jnp.float32) / HID
    base_draw = jnp.clip(jax.random.normal(key, (2, HID), jnp.float32), -4.0, 4.0)
    growth = 3.0 ** rising
    return (base_draw * growth[None, :] * HID ** (-0.5)).astype(jnp.bfloat16)


def with_ends(array, rng, low, high):
    longest = array.shape.index(max(array.shape))
    spots = []
    for shift in (0, 1):
        where = [jax.random.randint(jax.random.fold_in(rng, axis), (), 0, length) for axis, length in enumerate(array.shape)]
        where[longest] = (where[longest] + shift) % array.shape[longest]
        spots.append(tuple(where))
    return array.at[spots[0]].set(low).at[spots[1]].set(high)


def steps_of(rng, extent, cuts, smallest, top_value):
    factor_of = 1.0
    for axis_at, parts in cuts:
        steps = jax.random.uniform(jax.random.fold_in(jax.random.fold_in(rng, 6), axis_at), (parts,), jnp.float32, smallest / len(cuts), top_value / len(cuts))
        factor_of = factor_of * jnp.repeat(jnp.exp(steps), extent[axis_at] // parts).reshape((-1,) + (1,) * (len(extent) - 1 - axis_at))
    return factor_of


def normal_values(own_key, dims, deviation, bound, shards=(), held_as=jnp.bfloat16):
    level = steps_of(own_key, dims, shards, -0.22, 0.18) if shards else 1.0
    values = jax.random.normal(own_key, dims, jnp.float32) * deviation * level
    return jnp.minimum(jnp.maximum(values, -bound), bound).astype(held_as)


def setup_inputs(seed: int = 0, part: int = 0) -> dict:
    streams_of = jax.random.split(jax.random.key(seed), 8)
    own_keys = jax.random.split(jax.random.fold_in(streams_of[7], part), 8)
    return {
        "first_map": normal_values(own_keys[0], (NROWS, COLS, C), 1.0, 6.0, ((0, 16),)),
        "second_map": normal_values(own_keys[1], (NROWS, COLS, C), 1.0, 6.0, ((0, 16),)),
        "flow_target": normal_values(own_keys[2], (2, NROWS, COLS), 8.0, 48.0, ((1, 16),), jnp.float32),
        "valid_tiles": with_ends((jax.random.randint(own_keys[3], (NROWS // TILE, COLS // TILE), 0, 2) < 1).astype(jnp.int32), jax.random.fold_in(own_keys[3], 1), 0, 1),
        "conv_weight": normal_values(streams_of[4], (9, K, HID), (9 * K) ** -0.5, 0.21875),
        "conv_bias": normal_values(streams_of[5], (HID,), 0.5, 3.0, (), jnp.float32),
        "head_weight": draw_head_weight(jax.random.fold_in(streams_of[7], 71), part),
    }


clip_fraction = 0.25

def diagonals(products, window):
    leading = products.shape[:-2]
    block_width, wide_cols = (products.shape[-2], products.shape[-1])
    flattened = products.reshape(leading + (block_width * wide_cols,))
    flattened = jnp.concatenate([flattened, jnp.zeros(leading + (block_width,), flattened.dtype)], axis=-1)
    return flattened.reshape(leading + (block_width, wide_cols + 1))[..., :window]

def undiagonals(planes, wide_cols):
    leading = planes.shape[:-2]
    block_width, window = (planes.shape[-2], planes.shape[-1])
    filler = jnp.zeros(leading + (block_width, wide_cols + 1 - window), planes.dtype)
    padded = jnp.concatenate([planes, filler], axis=-1)
    flattened = padded.reshape(leading + (block_width * (wide_cols + 1),))[..., :block_width * wide_cols]
    return flattened.reshape(leading + (block_width, wide_cols))

def widen(padded, col_count, block_width):
    row_total, channels = (padded.shape[0], padded.shape[2])
    block_count = col_count // block_width
    main_part = padded[:, :col_count].reshape(row_total, block_count, block_width, channels)
    tail_part = padded[:, block_width:block_width + col_count].reshape(row_total, block_count, block_width, channels)
    return jnp.concatenate([main_part, tail_part[:, :, :2 * RADIUS]], axis=2)

def fold(wide_total, col_count, block_width):
    row_total, block_count, wide_cols, channels = wide_total.shape
    main_part = wide_total[:, :, :block_width].reshape(row_total, col_count, channels)
    tail_part = wide_total[:, :, block_width:]
    filler = jnp.zeros((row_total, block_count, 2 * block_width - wide_cols, channels), wide_total.dtype)
    tail_part = jnp.concatenate([tail_part, filler], axis=2).reshape(row_total, col_count, channels)
    folded = jnp.zeros((row_total, col_count + block_width, channels), wide_total.dtype)
    folded = folded.at[:, :col_count].add(main_part)
    return folded.at[:, block_width:].add(tail_part)

def reference(first_map, second_map, flow_target, valid_tiles, conv_weight, conv_bias, head_weight):
    row_count, col_count = (first_map.shape[0], first_map.shape[1])
    hidden_width = conv_weight.shape[2]
    window = 2 * RADIUS + 1
    block_width = math.gcd(col_count, 16)
    block_count = col_count // block_width
    wide_cols = block_width + 2 * RADIUS
    inverse_root = C ** (-0.5)
    second_pad = jnp.pad(second_map.astype(jnp.float32), ((RADIUS, RADIUS), (RADIUS, block_width - RADIUS), (0, 0)))
    second_wide = widen(second_pad, col_count, block_width)
    first_blocks = first_map.astype(jnp.float32).reshape(row_count, block_count, block_width, C)
    diagonal_list = []
    for vertical in range(window):
        products = jnp.einsum('rnic,rnjc->rnij', first_blocks, second_wide[vertical:vertical + row_count])
        diagonal_list.append(diagonals(products, window))
    correlation = jnp.concatenate(diagonal_list, axis=3).reshape(row_count, col_count, K)
    correlation = (correlation * inverse_root).astype(jnp.bfloat16)
    correlation = jnp.transpose(correlation, (0, 2, 1))
    corr_pad = jnp.pad(correlation, ((1, 1), (0, 0), (1, 1))).astype(jnp.float32)
    weight_float = conv_weight.astype(jnp.float32)
    preact = jnp.zeros((row_count, hidden_width, col_count), jnp.float32) + conv_bias[None, :, None]
    for offset in range(9):
        tap_row, tap_col = (offset // 3, offset % 3)
        window_corr = corr_pad[tap_row:tap_row + row_count, :, tap_col:tap_col + col_count]
        preact = preact + jnp.einsum('kh,rkw->rhw', weight_float[offset], window_corr)
    hidden = jax.nn.silu(preact).astype(jnp.bfloat16)
    hidden_float = hidden.astype(jnp.float32)
    head_float = head_weight.astype(jnp.float32)
    flow_pred = jnp.einsum('jh,rhw->jrw', head_float, hidden_float)
    cell_mask = jnp.repeat(jnp.repeat(valid_tiles, TILE, axis=0), TILE, axis=1).astype(jnp.float32)
    flow_error = (cell_mask[None] * (flow_pred - flow_target)).astype(jnp.bfloat16)
    error_float = flow_error.astype(jnp.float32)
    head_sum = jnp.einsum('jrw,rhw->jh', error_float, hidden_float)
    hidden_error = jnp.einsum('jh,jrw->rhw', head_float, error_float)
    sigmoid_pre = jax.nn.sigmoid(preact)
    preact_error = (hidden_error * sigmoid_pre * (1.0 + preact * (1.0 - sigmoid_pre))).astype(jnp.bfloat16)
    preact_float = preact_error.astype(jnp.float32)
    bias_sum = lax.optimization_barrier(jnp.sum(preact_float, axis=(0, 2)))
    error_pad = jnp.pad(preact_float, ((1, 1), (0, 0), (1, 1)))
    conv_list = []
    corr_error = jnp.zeros((row_count, K, col_count), jnp.float32)
    for offset in range(9):
        tap_row, tap_col = (offset // 3, offset % 3)
        window_corr = corr_pad[tap_row:tap_row + row_count, :, tap_col:tap_col + col_count]
        conv_list.append(jnp.einsum('rkw,rhw->kh', window_corr, preact_float))
        window_error = error_pad[2 - tap_row:2 - tap_row + row_count, :, 2 - tap_col:2 - tap_col + col_count]
        corr_error = corr_error + jnp.einsum('kh,rhw->rkw', weight_float[offset], window_error)
    conv_sum = jnp.stack(conv_list, axis=0)
    corr_error = (corr_error * inverse_root).astype(jnp.bfloat16)
    error_planes = jnp.transpose(corr_error, (0, 2, 1)).astype(jnp.float32)
    error_planes = error_planes.reshape(row_count, block_count, block_width, K)
    first_total = jnp.zeros((row_count, block_count, block_width, C), jnp.float32)
    second_total = jnp.zeros((row_count + 2 * RADIUS, block_count, wide_cols, C), jnp.float32)
    for vertical in range(window):
        spread = undiagonals(error_planes[..., vertical * window:(vertical + 1) * window], wide_cols)
        first_total = first_total + jnp.einsum('rnij,rnjc->rnic', spread, second_wide[vertical:vertical + row_count])
        second_total = second_total.at[vertical:vertical + row_count].add(jnp.einsum('rnij,rnic->rnjc', spread, first_blocks))
    first_total = first_total.reshape(row_count, col_count, C)
    second_fold = fold(second_total, col_count, block_width)[RADIUS:RADIUS + row_count, RADIUS:RADIUS + col_count]
    squares_all = jnp.sum(conv_sum * conv_sum) + jnp.sum(bias_sum * bias_sum) + jnp.sum(head_sum * head_sum)
    param_count = 9 * K * hidden_width + 3 * hidden_width
    clip_factor = jnp.minimum(1.0, clip_fraction * param_count ** 0.5 / jnp.sqrt(squares_all + 1e-06))
    return (first_total.astype(jnp.bfloat16), second_fold.astype(jnp.bfloat16), conv_sum * clip_factor, bias_sum * clip_factor, head_sum * clip_factor)
```

```python
import functools

import jax
import jax.numpy as jnp
from jax import lax
from jax.experimental import pallas as pl
from jax.experimental.pallas import tpu as pltpu
from jax.sharding import PartitionSpec as P

C = 256
RADIUS = 4
TILE = 16
K = 81
WIN = 9
LANES = 128

clip_fraction = 0.25

f32 = jnp.float32
bf16 = jnp.bfloat16

NT = (((1,), (1,)), ((), ()))
TN = (((0,), (0,)), ((), ()))


def dot(a, b, dims=None):
    if dims is None:
        return jnp.dot(a, b, preferred_element_type=f32)
    return lax.dot_general(a, b, dims, preferred_element_type=f32)


def iota(shape, dim):
    return lax.broadcasted_iota(jnp.int32, shape, dim)


def full(shape):
    return pl.BlockSpec(shape, lambda *_: (0,) * len(shape))


SMEM = pl.BlockSpec(memory_space=pltpu.SMEM)


def call(body, outs, args, scratch=(), specs=None):
    specs = specs or [full(a.shape) for a in args]
    return pl.pallas_call(
        body,
        out_shape=[jax.ShapeDtypeStruct(s, d) for s, d in outs],
        in_specs=specs,
        out_specs=[full(s) for s, _ in outs],
        scratch_shapes=list(scratch),
    )(*args)


def band_of(products, dyi):
    band = pltpu.roll(products, 8, 1, stride=1, stride_axis=0)[:, :LANES]
    return pltpu.roll(band, (9 * dyi - 3) % LANES, 1)


def spread_of(bands, dyi, cols):
    moved = pltpu.roll(bands, (4 - 9 * dyi) % LANES, 1)
    lane = iota(bands.shape, 1)
    own = jnp.where((lane >= 4) & (lane < 13), moved, 0.0)
    wide = jnp.concatenate([own, jnp.zeros((bands.shape[0], cols - LANES), own.dtype)], axis=1)
    return pltpu.roll(wide, cols - 8, 1, stride=1, stride_axis=0).astype(bf16)


def lane_valid(rows):
    lane = iota((rows, LANES), 1)
    col = iota((rows, LANES), 0) + lane % WIN - RADIUS
    return (col >= 0) & (col < rows) & (lane < K)


def corr_body(par_ref, first_ref, own_ref, low_ref, high_ref, corr_ref, ea_ref, eb_ref):
    rows, cols = first_ref.shape[0], first_ref.shape[1]
    par = par_ref[0]
    valid = lane_valid(cols)
    lane = iota((cols, LANES), 1)
    mirror = (iota((cols, cols), 0) + iota((cols, cols), 1) == cols - 1).astype(bf16)
    for r in range(rows):
        acc = jnp.zeros((cols, LANES), f32)
        turned = dot(mirror, first_ref[r]).astype(bf16)
        for dyi in range(WIN):
            q = r + dyi - RADIUS
            src = low_ref[q + RADIUS] if q < 0 else (high_ref[q - rows] if q >= rows else own_ref[q])
            band = band_of(dot(turned, src, NT), dyi)
            acc = jnp.where((lane >= 9 * dyi) & (lane < 9 * dyi + 9), band, acc)
        acc = dot(mirror, (acc * (C ** -0.5)).astype(bf16))
        acc = jnp.where(valid, acc, 0.0)
        acc = jnp.where(lane == K, 1.0, acc)
        corr_ref[r] = acc.astype(bf16)
    ea_ref[...] = corr_ref[(1 - par) * (rows - 1)]
    eb_ref[...] = corr_ref[par * (rows - 1)]


def shift_down(x, steps):
    zero = jnp.zeros((abs(steps), x.shape[1]), x.dtype)
    if steps > 0:
        return jnp.concatenate([zero, x[:-steps]], axis=0)
    return jnp.concatenate([x[-steps:], zero], axis=0)


def conv_body(par_ref, corr_ref, ha_ref, hb_ref, w_ref, bias_ref, head_ref, target_ref, mask_ref,
              pe_ref, pa_ref, pb_ref, sums_ref, x_ref, pt_ref):
    rows, cols = corr_ref.shape[0], corr_ref.shape[1]
    hid = w_ref.shape[2]
    par = par_ref[0]

    def put(slot, value):
        wide = value.astype(f32)
        x_ref[slot, :, 0:LANES] = shift_down(wide, 1).astype(bf16)
        x_ref[slot, :, LANES:2 * LANES] = value
        x_ref[slot, :, 2 * LANES:] = shift_down(wide, -1).astype(bf16)

    for r in range(rows):
        put(r + 1, corr_ref[r])
    put((1 - par) * (rows + 1), ha_ref[...])
    put(par * (rows + 1), hb_ref[...])
    head = head_ref[...]
    head_sum = jnp.zeros((head.shape[0], hid), f32)
    for r in range(rows):
        pre = bias_ref[...] + (dot(x_ref[r], w_ref[0]) + dot(x_ref[r + 1], w_ref[1]) + dot(x_ref[r + 2], w_ref[2]))
        sig = lax.logistic(pre)
        hidden = (pre * sig).astype(bf16)
        pred = dot(head, hidden, NT)
        err = mask_ref[pl.ds(r, 1), :] * (pred[0:2] - target_ref[:, r, :])
        err = jnp.concatenate([err, jnp.zeros((head.shape[0] - 2, cols), f32)], axis=0).astype(bf16)
        head_sum = head_sum + dot(err, hidden)
        herr = dot(err, head, TN)
        pe = (herr * sig * (1.0 + pre * (1.0 - sig))).astype(bf16)
        pe_ref[r] = pe
        pt_ref[:, r * cols:(r + 1) * cols] = pe.astype(f32).T.astype(bf16)
    pa_ref[...] = pe_ref[(1 - par) * (rows - 1)]
    pb_ref[...] = pe_ref[par * (rows - 1)]
    pieces = []
    bias_col = None
    for ty in range(3):
        x = x_ref[ty:ty + rows].reshape(rows * cols, 3 * LANES)
        part = dot(pt_ref[...], x)
        for tx in range(3):
            pieces.append(part[:, tx * LANES:tx * LANES + K])
        if ty == 1:
            bias_col = part[:, LANES + K:LANES + K + 1]
    head_cols = jnp.concatenate([head_sum, jnp.zeros((LANES - head.shape[0], hid), f32)], axis=0).T
    used = 9 * K + 3
    pad = jnp.zeros((hid, sums_ref.shape[1] - used), f32)
    sums_ref[...] = jnp.concatenate(pieces + [bias_col, head_cols[:, 0:2], pad], axis=1)


def cerr_body(par_ref, pe_ref, ha_ref, hb_ref, w_ref, ce_ref, ea_ref, eb_ref, ext_ref):
    rows, cols = pe_ref.shape[0], pe_ref.shape[1]
    par = par_ref[0]
    for r in range(rows):
        ext_ref[r + 1] = pe_ref[r]
    ext_ref[(1 - par) * (rows + 1)] = ha_ref[...]
    ext_ref[par * (rows + 1)] = hb_ref[...]
    valid = lane_valid(cols)
    lane = iota((cols, LANES), 1)
    to_low = jnp.zeros((cols, LANES), f32)
    to_high = jnp.zeros((cols, LANES), f32)
    low_at = high_at = 0
    for r in range(rows):
        z = dot(ext_ref[r + 2], w_ref[0], NT) + dot(ext_ref[r + 1], w_ref[1], NT) + dot(ext_ref[r], w_ref[2], NT)
        total = shift_down(z[:, 0:LANES], -1) + z[:, LANES:2 * LANES] + shift_down(z[:, 2 * LANES:], 1)
        total = jnp.where(valid, total * (C ** -0.5), 0.0)
        ce_ref[r] = total.astype(bf16)
        count = 9 * (RADIUS - r)
        moved = pltpu.roll(total, low_at, 1) if low_at else total
        to_low = jnp.where((lane >= low_at) & (lane < low_at + count), moved, to_low)
        low_at += count
        count = 9 * (r + 1 + RADIUS - rows)
        start = K - count
        moved = pltpu.roll(total, (high_at - start) % LANES, 1)
        to_high = jnp.where((lane >= high_at) & (lane < high_at + count), moved, to_high)
        high_at += count
    up = to_low.astype(bf16)
    down = to_high.astype(bf16)

    @pl.when(par == 0)
    def _():
        ea_ref[...] = down
        eb_ref[...] = up

    @pl.when(par != 0)
    def _():
        ea_ref[...] = up
        eb_ref[...] = down


def own_grad_body(ce_ref, first_ref, second_ref, low_ref, high_ref, fg_ref, part_ref):
    rows, cols = ce_ref.shape[0], ce_ref.shape[1]
    parts = [jnp.zeros((cols, C), f32) for _ in range(rows)]
    for r in range(rows):
        bands = ce_ref[r].astype(f32)
        acc = jnp.zeros((cols, C), f32)
        for dyi in range(WIN):
            q = r + dyi - RADIUS
            src = low_ref[q + RADIUS] if q < 0 else (high_ref[q - rows] if q >= rows else second_ref[q])
            spread = spread_of(bands, dyi, cols)
            acc = acc + dot(spread, src)
            if 0 <= q < rows:
                parts[q] = parts[q] + dot(spread, first_ref[r], TN)
        fg_ref[r] = acc.astype(bf16)
    for r in range(rows):
        part_ref[r] = parts[r]


def halo_grad_body(par_ref, part_ref, ca_ref, cb_ref, low_ref, high_ref, sg_ref, c_ref):
    rows, cols = part_ref.shape[0], part_ref.shape[1]
    par = par_ref[0]
    c_ref[1 - par] = ca_ref[...].astype(f32)
    c_ref[par] = cb_ref[...].astype(f32)
    parts = [part_ref[r] for r in range(rows)]
    above = c_ref[0]
    below = c_ref[1]
    at = 0
    for a in range(rows):
        for i, dy in enumerate(range(rows - a, RADIUS + 1)):
            spread = spread_of(above, at // 9 + i, cols)
            q = a + dy - rows
            parts[q] = parts[q] + dot(spread, low_ref[a], TN)
        at += 9 * (RADIUS + 1 - rows + a)
    at = 0
    for b in range(rows):
        for i, dy in enumerate(range(-RADIUS, -b)):
            spread = spread_of(below, at // 9 + i, cols)
            q = rows + b + dy
            parts[q] = parts[q] + dot(spread, high_ref[b], TN)
        at += 9 * (RADIUS - b)
    for r in range(rows):
        sg_ref[r] = parts[r].astype(bf16)


def final_body(sq_ref, piece_ref, conv_ref, bias_ref, head_ref, *, limit):
    factor = jnp.minimum(1.0, limit / jnp.sqrt(sq_ref[0:1, 0:1] + 1e-06))
    piece = piece_ref[...] * factor
    share = conv_ref.shape[2]
    height = -(-piece.shape[0] // LANES) * LANES
    if height != piece.shape[0]:
        piece = jnp.concatenate([piece, jnp.zeros((height - piece.shape[0], piece.shape[1]), f32)], axis=0)
    turned = piece.T
    for tap in range(9):
        conv_ref[tap] = turned[tap * K:(tap + 1) * K, 0:share]
    bias_ref[...] = turned[9 * K:9 * K + 1, 0:share]
    head_ref[...] = turned[9 * K + 1:9 * K + 3, 0:share]


def square_body(piece_ref, out_ref):
    piece = piece_ref[...]
    out_ref[...] = jnp.broadcast_to(jnp.sum(piece * piece).reshape(1, 1), out_ref.shape)


def on_device(first_map, second_map, flow_target, valid_tiles, conv_weight, conv_bias, head_weight):
    rows, cols = first_map.shape[0], first_map.shape[1]
    hid = conv_weight.shape[2]
    count = lax.axis_size("region")
    index = lax.axis_index("region")
    par = (index % 2).reshape(1)
    forward = [(i, i + 1) for i in range(count - 1)]
    backward = [(b, a) for a, b in forward]
    inner = [(i, i ^ 1) for i in range(count)]
    outer = [(i, i + 1) for i in range(1, count - 1, 2)]
    outer = outer + [(b, a) for a, b in outer]

    def permute(x, pairs):
        return lax.ppermute(x, "region", pairs)

    second_low = permute(second_map, forward)
    second_high = permute(second_map, backward)

    share = hid // count
    radix = [2] * (count.bit_length() - 1)
    turn = tuple(reversed(range(len(radix)))) + (len(radix),)

    def reorder(x):
        return jnp.transpose(x.reshape(tuple(radix) + (share,)), turn).reshape(hid)

    order = reorder(jnp.arange(hid))
    select = (jnp.arange(hid)[:, None] == order[None, :]).astype(bf16)
    weight = jnp.einsum("tkh,hg->tkg", conv_weight, select, preferred_element_type=bf16)
    weight = jnp.pad(weight, ((0, 0), (0, LANES - K), (0, 0))).reshape(3, 3 * LANES, hid)
    head = jnp.einsum("jh,hg->jg", head_weight, select, preferred_element_type=bf16)
    head = jnp.pad(head, ((0, 14), (0, 0)))
    bias = reorder(conv_bias).reshape(1, hid)
    tile_rows = jnp.repeat(valid_tiles, TILE, axis=0)
    own_tiles = lax.dynamic_slice_in_dim(tile_rows, index * rows, rows, 0)
    mask = jnp.repeat(own_tiles, TILE, axis=1).astype(f32)

    vector = lambda *s: pltpu.VMEM(s, bf16)
    corr, edge_a, edge_b = call(
        corr_body,
        [((rows, cols, LANES), bf16), ((cols, LANES), bf16), ((cols, LANES), bf16)],
        (par, first_map, second_map, second_low, second_high),
        specs=[SMEM, full(first_map.shape)] + [full(second_map.shape), full(second_low.shape), full(second_high.shape)],
    )
    halo_a = permute(edge_a, inner)
    halo_b = permute(edge_b, outer)
    args = (par, corr, halo_a, halo_b, weight, bias, head, flow_target, mask)
    pe, pe_a, pe_b, sums = call(
        conv_body,
        [((rows, cols, hid), bf16), ((cols, hid), bf16), ((cols, hid), bf16), ((hid, 768), f32)],
        args,
        scratch=[vector(rows + 2, cols, 3 * LANES), vector(hid, rows * cols)],
        specs=[SMEM] + [full(a.shape) for a in args[1:]],
    )
    pe_halo_a = permute(pe_a, inner)
    pe_halo_b = permute(pe_b, outer)

    piece = sums
    early = None
    for step in range(len(radix)):
        half = piece.shape[0] // 2
        bit = (index >> step) & 1
        halves = piece.reshape(2, half, piece.shape[1])
        keep = lax.dynamic_index_in_dim(halves, bit, 0, False)
        send = lax.dynamic_index_in_dim(halves, 1 - bit, 0, False)
        piece = keep + permute(send, [(i, i ^ (1 << step)) for i in range(count)])
        if step == 1:
            early = piece

    first_tied, _ = lax.optimization_barrier((first_map, early))
    first_low = permute(first_tied, forward)
    first_high = permute(first_tied, backward)

    args = (par, pe, pe_halo_a, pe_halo_b, weight)
    cerr, ce_a, ce_b = call(
        cerr_body,
        [((rows, cols, LANES), bf16), ((cols, LANES), bf16), ((cols, LANES), bf16)],
        args,
        scratch=[vector(rows + 2, cols, hid)],
        specs=[SMEM] + [full(a.shape) for a in args[1:]],
    )
    ce_halo_a = permute(ce_a, inner)
    ce_halo_b = permute(ce_b, outer)
    first_grad, part = call(
        own_grad_body,
        [((rows, cols, C), bf16), ((rows, cols, C), f32)],
        (cerr, first_map, second_map, second_low, second_high),
    )
    args = (par, part, ce_halo_a, ce_halo_b, first_low, first_high)
    (second_grad,) = call(
        halo_grad_body,
        [((rows, cols, C), bf16)],
        args,
        scratch=[pltpu.VMEM((2, cols, LANES), f32)],
        specs=[SMEM] + [full(a.shape) for a in args[1:]],
    )

    (square,) = call(square_body, [((8, LANES), f32)], (piece,))
    for step in range(len(radix)):
        square = square + permute(square, [(i, i ^ (1 << step)) for i in range(count)])
    param_count = 9 * K * hid + 3 * hid
    conv_piece, bias_piece, head_piece = call(
        functools.partial(final_body, limit=clip_fraction * param_count ** 0.5),
        [((9, K, share), f32), ((1, share), f32), ((2, share), f32)],
        (square, piece),
    )
    return first_grad, second_grad, conv_piece, bias_piece.reshape(share), head_piece


def solution(mesh):
    return jax.shard_map(
        on_device,
        mesh=mesh,
        in_specs=(
            P("region", "group", None),
            P("region", "group", None),
            P(None, "region", "group"),
            P(None, "group"),
            P(),
            P(),
            P(),
        ),
        out_specs=(
            P("region", "group", None),
            P("region", "group", None),
            P("group", None, "region"),
            P(("group", "region")),
            P("group", "region"),
        ),
        check_vma=False,
    )
```

```python
import functools

import jax
import jax.numpy as jnp
from jax import lax
from jax.experimental import pallas as pl
from jax.experimental.pallas import tpu as pltpu
from jax.sharding import PartitionSpec as P

C = 256
RADIUS = 4
TILE = 16
K = 81
WIN = 9
LANES = 128

clip_fraction = 0.25
WIDTH = 768
VMEM_LIMIT = 24 * 1024 * 1024

f32 = jnp.float32
bf16 = jnp.bfloat16

NT = (((1,), (1,)), ((), ()))
TN = (((0,), (0,)), ((), ()))


def dot(a, b, dims=None):
    if dims is None:
        return jnp.dot(a, b, preferred_element_type=f32)
    return lax.dot_general(a, b, dims, preferred_element_type=f32)


def iota(shape, dim):
    return lax.broadcasted_iota(jnp.int32, shape, dim)


SMEM = pl.BlockSpec(memory_space=pltpu.SMEM)
VMEM = pl.BlockSpec(memory_space=pltpu.VMEM)


def call(body, outs, args, scratch=(), scalar=False):
    specs = [VMEM] * len(args)
    if scalar:
        specs[0] = SMEM
    return pl.pallas_call(
        body,
        out_shape=[jax.ShapeDtypeStruct(s, d) for s, d in outs],
        in_specs=specs,
        out_specs=[VMEM] * len(outs),
        scratch_shapes=list(scratch),
        compiler_params=pltpu.CompilerParams(vmem_limit_bytes=VMEM_LIMIT),
    )(*args)


def after(value, *others):
    return lax.optimization_barrier((value,) + others)[0]


HALF = LANES


def band_of(products, dyi):
    lane = iota((8, HALF), 1)
    near = jnp.where(lane >= HALF - 8, products[HALF - 8:HALF, :HALF], products[HALF - 8:HALF, HALF:])
    far = jnp.where(lane < 8, products[HALF:HALF + 8, HALF:], products[HALF:HALF + 8, :HALF])
    ring = jnp.concatenate([products[:HALF - 8, HALF:], near, far, products[HALF + 8:, :HALF]], axis=0)
    band = pltpu.roll(ring, 8, 1, stride=1, stride_axis=0)
    return pltpu.roll(band, (9 * dyi - 3) % LANES, 1)


def spread_of(bands, dyi):
    moved = pltpu.roll(bands, (4 - 9 * dyi) % LANES, 1)
    lane = iota(bands.shape, 1)
    own = jnp.where((lane >= 4) & (lane < 13), moved, 0.0)
    ring = pltpu.roll(own, HALF - 8, 1, stride=1, stride_axis=0)
    edge = iota((8, HALF), 1)
    none = jnp.zeros((8, HALF), f32)
    near = ring[HALF - 8:HALF]
    far = ring[HALF:HALF + 8]
    left = jnp.concatenate([ring[HALF - 16:HALF - 8], jnp.where(edge < 8, 0.0, near), jnp.where(edge >= HALF - 8, far, 0.0), none], axis=0)
    right = jnp.concatenate([none, jnp.where(edge < 8, near, 0.0), jnp.where(edge >= HALF - 8, 0.0, far), ring[HALF + 8:HALF + 16]], axis=0)
    zero = jnp.zeros((HALF - 16, HALF), bf16)
    left = jnp.concatenate([ring[:HALF - 16].astype(bf16), left.astype(bf16), zero], axis=0)
    right = jnp.concatenate([zero, right.astype(bf16), ring[HALF + 16:].astype(bf16)], axis=0)
    return jnp.concatenate([left, right], axis=1)


def lane_valid(rows):
    lane = iota((rows, LANES), 1)
    col = iota((rows, LANES), 0) + lane % WIN - RADIUS
    return (col >= 0) & (col < rows) & (lane < K)


def corr_rows(first_ref, second_ref, start, before, put):
    rows, cols = first_ref.shape[0], first_ref.shape[1]
    count = second_ref.shape[0]
    lane = iota((cols, LANES), 1)
    valid = lane_valid(cols)
    mirror = (iota((cols, cols), 0) + iota((cols, cols), 1) == cols - 1).astype(bf16)
    for r in range(rows):
        dys = [q - r + RADIUS for q in range(start, start + count) if abs(q - r) <= RADIUS]
        if not dys:
            put(r, before[r])
            continue
        turned = dot(mirror, first_ref[r]).astype(bf16)
        acc = jnp.zeros((cols, LANES), f32)
        for dyi in dys:
            band = band_of(dot(turned, second_ref[r + dyi - RADIUS - start], NT), dyi)
            acc = jnp.where((lane >= 9 * dyi) & (lane < 9 * dyi + 9), band, acc)
        acc = jnp.where(valid, dot(mirror, (acc * (C ** -0.5)).astype(bf16)), 0.0)
        if before is None:
            acc = jnp.where(lane == K, 1.0, acc)
        else:
            inside = (lane >= 9 * dys[0]) & (lane < 9 * dys[-1] + 9)
            acc = jnp.where(inside, acc, before[r].astype(f32))
        put(r, acc.astype(bf16))


def corr_own_body(first_ref, own_ref, corr_ref):
    corr_rows(first_ref, own_ref, 0, None, lambda r, v: corr_ref.__setitem__(r, v))


def corr_halo_body(par_ref, first_ref, old_ref, low_ref, high_ref, corr_ref, ea_ref, eb_ref, mid_ref):
    rows = first_ref.shape[0]
    par = par_ref[0]
    corr_rows(first_ref, low_ref, -low_ref.shape[0], old_ref, lambda r, v: mid_ref.__setitem__(r, v))
    corr_rows(first_ref, high_ref, rows, mid_ref, lambda r, v: corr_ref.__setitem__(r, v))
    ea_ref[...] = corr_ref[(1 - par) * (rows - 1)]
    eb_ref[...] = corr_ref[par * (rows - 1)]


def shift_down(x, steps):
    zero = jnp.zeros((abs(steps), x.shape[1]), x.dtype)
    if steps > 0:
        return jnp.concatenate([zero, x[:-steps]], axis=0)
    return jnp.concatenate([x[-steps:], zero], axis=0)


def put_taps(x_ref, slot, value):
    wide = value.astype(f32)
    x_ref[slot, :, 0:LANES] = shift_down(wide, 1).astype(bf16)
    x_ref[slot, :, LANES:2 * LANES] = value
    x_ref[slot, :, 2 * LANES:] = shift_down(wide, -1).astype(bf16)


def cell_row(pre, r, head, target_ref, mask_ref):
    cols = pre.shape[0]
    sig = lax.logistic(pre)
    hidden = (pre * sig).astype(bf16)
    pred = dot(head, hidden, NT)
    err = mask_ref[r:r + 1, :] * (pred[0:2] - target_ref[:, r, :])
    err = jnp.concatenate([err, jnp.zeros((head.shape[0] - 2, cols), f32)], axis=0).astype(bf16)
    herr = dot(err, head, TN)
    pe = (herr * sig * (1.0 + pre * (1.0 - sig))).astype(bf16)
    return pe, dot(err, hidden)


def conv_own_body(corr_ref, w_ref, bias_ref, head_ref, target_ref, mask_ref, x_ref, pre_ref, pe_ref, part_ref, hsum_ref, pt_ref):
    rows, cols = corr_ref.shape[0], corr_ref.shape[1]
    for r in range(rows):
        put_taps(x_ref, r, corr_ref[r])
    head = head_ref[...]
    pre_ref[0] = bias_ref[...] + (dot(x_ref[0], w_ref[1]) + dot(x_ref[1], w_ref[2]))
    pre_ref[1] = bias_ref[...] + (dot(x_ref[rows - 2], w_ref[0]) + dot(x_ref[rows - 1], w_ref[1]))
    total = jnp.zeros(hsum_ref.shape, f32)
    for r in range(1, rows - 1):
        pre = bias_ref[...] + (dot(x_ref[r - 1], w_ref[0]) + dot(x_ref[r], w_ref[1]) + dot(x_ref[r + 1], w_ref[2]))
        pe, head_sum = cell_row(pre, r, head, target_ref, mask_ref)
        total = total + head_sum
        pe_ref[r - 1] = pe
        pt_ref[:, (r - 1) * cols:r * cols] = pe.T
    hsum_ref[...] = total
    for ty in range(3):
        x = x_ref[ty:ty + rows - 2].reshape((rows - 2) * cols, 3 * LANES)
        part_ref[:, ty * 3 * LANES:(ty + 1) * 3 * LANES] = dot(pt_ref[...], x)


def conv_edge_body(par_ref, x_ref, pre_ref, part_ref, hsum_ref, ha_ref, hb_ref, w_ref, head_ref, target_ref, mask_ref,
                   pe_ref, pa_ref, pb_ref, keep_ref, send_ref, h_ref, pt_ref):
    rows, cols = x_ref.shape[0], x_ref.shape[1]
    hid = w_ref.shape[2]
    par = par_ref[0]
    put_taps(h_ref, 1 - par, ha_ref[...])
    put_taps(h_ref, par, hb_ref[...])
    head = head_ref[...]
    head_sum = hsum_ref[...]
    for i, r in enumerate((0, rows - 1)):
        pre = pre_ref[i] + dot(h_ref[i], w_ref[2 * i])
        pe, own_sum = cell_row(pre, r, head, target_ref, mask_ref)
        head_sum = head_sum + own_sum
        pe_ref[i] = pe
        pt_ref[i] = pe.T
    pa_ref[...] = pe_ref[1 - par]
    pb_ref[...] = pe_ref[par]
    top, bottom = pt_ref[0], pt_ref[1]
    pieces = []
    bias_col = None
    for ty in range(3):
        low = h_ref[0] if ty == 0 else x_ref[ty - 1]
        high = h_ref[1] if ty == 2 else x_ref[rows - 2 + ty]
        part = part_ref[:, ty * 3 * LANES:(ty + 1) * 3 * LANES] + (dot(top, low) + dot(bottom, high))
        for tx in range(3):
            pieces.append(part[:, tx * LANES:tx * LANES + K])
        if ty == 1:
            bias_col = part[:, LANES + K:LANES + K + 1]
    head_cols = jnp.concatenate([head_sum, jnp.zeros((LANES - head.shape[0], hid), f32)], axis=0).T
    pad = jnp.zeros((hid, WIDTH - 9 * K - 3), f32)
    sums = jnp.concatenate(pieces + [bias_col, head_cols[:, 0:2], pad], axis=1)
    upper, lower = sums[:hid // 2], sums[hid // 2:]
    keep_ref[...] = jnp.where(par == 0, upper, lower)
    send_ref[...] = jnp.where(par == 0, lower, upper)


def halve_body(bit_ref, own_ref, got_ref, keep_ref, send_ref):
    half = keep_ref.shape[0]
    bit = bit_ref[0]
    upper = own_ref[:half] + got_ref[:half]
    lower = own_ref[half:] + got_ref[half:]
    keep_ref[...] = jnp.where(bit == 0, upper, lower)
    send_ref[...] = jnp.where(bit == 0, lower, upper)


def tail_body(own_ref, got_ref, conv_ref, rest_ref, square_ref):
    piece = own_ref[...] + got_ref[...]
    share = piece.shape[0]
    for tap in range(9):
        conv_ref[tap] = piece[:, tap * K:(tap + 1) * K]
    start = 9 * K // LANES * LANES
    rest = jnp.concatenate([piece[:, start:start + LANES], jnp.zeros((LANES - share, LANES), f32)], axis=0)
    rest_ref[...] = rest.T[9 * K - start:9 * K - start + 3, 0:share]
    square_ref[...] = jnp.broadcast_to(jnp.sum(piece * piece).reshape(1, 1), square_ref.shape)


def final_body(sq_ref, got_ref, conv_ref, rest_ref, out_ref, bias_ref, head_ref, *, limit):
    factor = jnp.minimum(1.0, limit / jnp.sqrt(sq_ref[0:1, 0:1] + got_ref[0:1, 0:1] + 1e-06))
    out_ref[...] = conv_ref[...] * factor.reshape(1, 1, 1)
    bias_ref[...] = rest_ref[0:1] * factor
    head_ref[...] = rest_ref[1:3] * factor


def cerr_row(z0, z1, z2):
    z = z0 + z1 + z2
    return shift_down(z[:, 0:LANES], -1) + z[:, LANES:2 * LANES] + shift_down(z[:, 2 * LANES:], 1)


def cerr_own_body(mid_ref, edge_ref, w_ref, ce_ref, rest_ref):
    rows = mid_ref.shape[0] + 2
    cols = mid_ref.shape[1]
    valid = lane_valid(cols)
    row = lambda r: edge_ref[0] if r == 0 else (edge_ref[1] if r == rows - 1 else mid_ref[r - 1])
    for r in range(rows):
        parts = [dot(row(r + 1 - ty), w_ref[ty], NT) for ty in range(3) if 0 <= r + 1 - ty < rows]
        total = cerr_row(parts[0], parts[1], parts[2] if len(parts) == 3 else 0.0)
        if 0 < r < rows - 1:
            ce_ref[r - 1] = jnp.where(valid, total * (C ** -0.5), 0.0).astype(bf16)
        else:
            rest_ref[min(r, 1)] = total


def cerr_edge_body(par_ref, mid_ref, rest_ref, ha_ref, hb_ref, w_ref, ce_ref, ea_ref, eb_ref, h_ref):
    rows = mid_ref.shape[0] + 2
    cols = mid_ref.shape[1]
    par = par_ref[0]
    h_ref[1 - par] = ha_ref[...]
    h_ref[par] = hb_ref[...]
    valid = lane_valid(cols)
    lane = iota((cols, LANES), 1)
    for i in range(2):
        total = rest_ref[i] + cerr_row(dot(h_ref[i], w_ref[2 - 2 * i], NT), 0.0, 0.0)
        ce_ref[i] = jnp.where(valid, total * (C ** -0.5), 0.0).astype(bf16)
    to_low = jnp.zeros((cols, LANES), f32)
    to_high = jnp.zeros((cols, LANES), f32)
    low_at = high_at = 0
    for r in range(rows):
        total = (ce_ref[min(r, 1)] if r in (0, rows - 1) else mid_ref[r - 1]).astype(f32)
        count = 9 * (RADIUS - r)
        moved = pltpu.roll(total, low_at, 1) if low_at else total
        to_low = jnp.where((lane >= low_at) & (lane < low_at + count), moved, to_low)
        low_at += count
        count = 9 * (r + 1 + RADIUS - rows)
        start = K - count
        moved = pltpu.roll(total, (high_at - start) % LANES, 1)
        to_high = jnp.where((lane >= high_at) & (lane < high_at + count), moved, to_high)
        high_at += count
    up = to_low.astype(bf16)
    down = to_high.astype(bf16)

    @pl.when(par == 0)
    def _():
        ea_ref[...] = down
        eb_ref[...] = up

    @pl.when(par != 0)
    def _():
        ea_ref[...] = up
        eb_ref[...] = down


def row_grad(cerr, own_rows, first_ref, second_ref, low_ref, high_ref, fg_ref, part_ref, old_ref):
    rows, cols = first_ref.shape[0], first_ref.shape[1]
    parts = [None if old_ref is None else old_ref[q] for q in range(rows)]
    for i, r in enumerate(own_rows):
        bands = cerr[i].astype(f32)
        turned = first_ref[r].T
        acc = jnp.zeros((cols, C), f32)
        for dyi in range(WIN):
            q = r + dyi - RADIUS
            src = low_ref[q + RADIUS] if q < 0 else (high_ref[q - rows] if q >= rows else second_ref[q])
            spread = spread_of(bands, dyi)
            acc = acc + dot(spread, src)
            if 0 <= q < rows:
                gave = dot(turned, spread)
                parts[q] = gave if parts[q] is None else parts[q] + gave
        fg_ref[i] = acc.astype(bf16)
    for q in range(rows):
        part_ref[q] = parts[q]


def mid_grad_body(ce_ref, first_ref, second_ref, low_ref, high_ref, fg_ref, part_ref):
    row_grad(ce_ref, range(1, first_ref.shape[0] - 1), first_ref, second_ref, low_ref, high_ref, fg_ref, part_ref, None)


def edge_grad_body(ce_ref, old_ref, first_ref, second_ref, low_ref, high_ref, fg_ref, part_ref):
    row_grad(ce_ref, (0, first_ref.shape[0] - 1), first_ref, second_ref, low_ref, high_ref, fg_ref, part_ref, old_ref)


def halo_grad_body(par_ref, part_ref, ca_ref, cb_ref, low_ref, high_ref, sg_ref, c_ref):
    rows, cols = part_ref.shape[0], part_ref.shape[2]
    par = par_ref[0]
    c_ref[1 - par] = ca_ref[...].astype(f32)
    c_ref[par] = cb_ref[...].astype(f32)
    parts = [part_ref[r] for r in range(rows)]
    above = c_ref[0]
    below = c_ref[1]
    at = 0
    for a in range(rows):
        turned = low_ref[a].T
        for i, dy in enumerate(range(rows - a, RADIUS + 1)):
            q = a + dy - rows
            parts[q] = parts[q] + dot(turned, spread_of(above, at // 9 + i))
        at += 9 * (RADIUS + 1 - rows + a)
    at = 0
    for b in range(rows):
        turned = high_ref[b].T
        for i, dy in enumerate(range(-RADIUS, -b)):
            q = rows + b + dy
            parts[q] = parts[q] + dot(turned, spread_of(below, at // 9 + i))
        at += 9 * (RADIUS - b)
    for r in range(rows):
        sg_ref[r] = parts[r].T.astype(bf16)


def on_device(first_map, second_map, flow_target, valid_tiles, conv_weight, conv_bias, head_weight):
    rows, cols = first_map.shape[0], first_map.shape[1]
    hid = conv_weight.shape[2]
    count = lax.axis_size("region")
    index = lax.axis_index("region")
    par = (index % 2).reshape(1)
    forward = [(i, i + 1) for i in range(count - 1)]
    backward = [(b, a) for a, b in forward]
    inner = [(i, i ^ 1) for i in range(count)]
    outer = [(i, i + 1) for i in range(1, count - 1, 2)]
    outer = outer + [(b, a) for a, b in outer]

    def permute(x, pairs):
        return lax.ppermute(x, "region", pairs)

    def swap(x, step):
        return permute(x, [(i, i ^ (1 << step)) for i in range(count)])

    second_low = permute(second_map, forward)
    second_high = permute(second_map, backward)

    share = hid // count
    radix = [2] * (count.bit_length() - 1)
    turn = tuple(reversed(range(len(radix)))) + (len(radix),)

    def reorder(x):
        return jnp.transpose(x.reshape(tuple(radix) + (share,)), turn).reshape(hid)

    order = reorder(jnp.arange(hid))
    select = (jnp.arange(hid)[:, None] == order[None, :]).astype(bf16)
    weight = jnp.einsum("tkh,hg->tkg", conv_weight, select, preferred_element_type=bf16)
    weight = jnp.pad(weight, ((0, 0), (0, LANES - K), (0, 0))).reshape(3, 3 * LANES, hid)
    head = jnp.einsum("jh,hg->jg", head_weight, select, preferred_element_type=bf16)
    head = jnp.pad(head, ((0, 14), (0, 0)))
    bias = reorder(conv_bias).reshape(1, hid)
    tile_rows = jnp.repeat(valid_tiles, TILE, axis=0)
    own_tiles = lax.dynamic_slice_in_dim(tile_rows, index * rows, rows, 0)
    mask = jnp.repeat(own_tiles, TILE, axis=1).astype(f32)

    vector = lambda *s: pltpu.VMEM(s, bf16)
    (corr_own,) = call(corr_own_body, [((rows, cols, LANES), bf16)], (first_map, second_map))
    weight, head, bias, mask, corr_own, second_low, second_high = lax.optimization_barrier(
        (weight, head, bias, mask, corr_own, second_low, second_high)
    )
    corr, edge_a, edge_b = call(
        corr_halo_body,
        [((rows, cols, LANES), bf16), ((cols, LANES), bf16), ((cols, LANES), bf16)],
        (par, first_map, corr_own, second_low, second_high),
        scratch=[vector(rows, cols, LANES)],
        scalar=True,
    )
    halo_a = permute(edge_a, inner)
    halo_b = permute(edge_b, outer)
    taps, pre_edge, pe_mid, part_sums, head_part = call(
        conv_own_body,
        [((rows, cols, 3 * LANES), bf16), ((2, cols, hid), f32), ((rows - 2, cols, hid), bf16), ((hid, 9 * LANES), f32), ((16, hid), f32)],
        (corr, weight, bias, head, flow_target, mask),
        scratch=[vector(hid, (rows - 2) * cols)],
    )
    halo_a, halo_b, taps = lax.optimization_barrier((halo_a, halo_b, taps))
    pe_edge, pe_a, pe_b, keep, send = call(
        conv_edge_body,
        [((2, cols, hid), bf16), ((cols, hid), bf16), ((cols, hid), bf16), ((hid // 2, WIDTH), f32), ((hid // 2, WIDTH), f32)],
        (par, taps, pre_edge, part_sums, head_part, halo_a, halo_b, weight, head, flow_target, mask),
        scratch=[vector(2, cols, 3 * LANES), vector(2, hid, cols)],
        scalar=True,
    )
    got = swap(send, 0)
    pe_halo_a = permute(pe_a, inner)
    pe_halo_b = permute(pe_b, outer)

    def halve(step, keep, got):
        half = keep.shape[0] // 2
        bit = ((index >> step) & 1).reshape(1)
        return call(halve_body, [((half, WIDTH), f32)] * 2, (bit, keep, got), scalar=True)

    keep, send = halve(1, keep, got)
    got = swap(send, 1)
    ce_mid, ce_rest = call(
        cerr_own_body,
        [((rows - 2, cols, LANES), bf16), ((2, cols, LANES), f32)],
        (pe_mid, pe_edge, weight),
    )
    mid_grad, part = call(
        mid_grad_body,
        [((rows - 2, cols, C), bf16), ((rows, C, cols), f32)],
        (after(ce_mid, send), first_map, second_map, second_low, second_high),
    )
    got, part = lax.optimization_barrier((got, part))
    keep, send = halve(2, keep, got)
    got = swap(send, 2)
    first_tied = after(first_map, send)
    first_low = permute(first_tied, forward)
    first_high = permute(first_tied, backward)
    ce_edge, ce_a, ce_b = call(
        cerr_edge_body,
        [((2, cols, LANES), bf16), ((cols, LANES), bf16), ((cols, LANES), bf16)],
        (par, ce_mid, after(ce_rest, send), pe_halo_a, pe_halo_b, weight),
        scratch=[vector(2, cols, hid)],
        scalar=True,
    )
    ce_halo_a = permute(ce_a, inner)
    ce_halo_b = permute(ce_b, outer)
    got, ce_edge = lax.optimization_barrier((got, ce_edge))
    for step in range(3, len(radix)):
        keep, send = halve(step, keep, got)
        got = swap(send, step)
    edge_grad, part = call(
        edge_grad_body,
        [((2, cols, C), bf16), ((rows, C, cols), f32)],
        (after(ce_edge, send), part, first_map, second_map, second_low, second_high),
    )
    got, part = lax.optimization_barrier((got, part))
    conv_raw, rest_raw, square = call(
        tail_body,
        [((9, share, K), f32), ((3, share), f32), ((8, LANES), f32)],
        (keep, got),
    )
    (second_grad,) = call(
        halo_grad_body,
        [((rows, cols, C), bf16)],
        (par, part, ce_halo_a, ce_halo_b, first_low, first_high),
        scratch=[pltpu.VMEM((2, cols, LANES), f32)],
        scalar=True,
    )
    got = swap(square, 0)
    for step in range(1, len(radix)):
        square = square + got
        got = swap(square, step)
    param_count = 9 * K * hid + 3 * hid
    conv_piece, bias_piece, head_piece = call(
        functools.partial(final_body, limit=clip_fraction * param_count ** 0.5),
        [((9, share, K), f32), ((1, share), f32), ((2, share), f32)],
        (square, got, conv_raw, rest_raw),
    )
    first_grad = jnp.concatenate([edge_grad[:1], mid_grad, edge_grad[1:]], axis=0)
    return first_grad, second_grad, jnp.transpose(conv_piece, (0, 2, 1)), bias_piece.reshape(share), head_piece


def solution(mesh):
    return jax.shard_map(
        on_device,
        mesh=mesh,
        in_specs=(
            P("region", "group", None),
            P("region", "group", None),
            P(None, "region", "group"),
            P(None, "group"),
            P(),
            P(),
            P(),
        ),
        out_specs=(
            P("region", "group", None),
            P("region", "group", None),
            P("group", None, "region"),
            P(("group", "region")),
            P("group", "region"),
        ),
        check_vma=False,
    )
```

```python
import functools

import jax
import jax.numpy as jnp
from jax import lax
from jax.experimental import pallas as pl
from jax.experimental.pallas import tpu as pltpu
from jax.sharding import PartitionSpec as P

C = 256
RADIUS = 4
TILE = 16
K = 81
WIN = 9
LANES = 128

clip_fraction = 0.25
WIDTH = 768
VMEM_LIMIT = 24 * 1024 * 1024

f32 = jnp.float32
bf16 = jnp.bfloat16

NT = (((1,), (1,)), ((), ()))
TN = (((0,), (0,)), ((), ()))


def dot(a, b, dims=None):
    if dims is None:
        return jnp.dot(a, b, preferred_element_type=f32)
    return lax.dot_general(a, b, dims, preferred_element_type=f32)


def iota(shape, dim):
    return lax.broadcasted_iota(jnp.int32, shape, dim)


SMEM = pl.BlockSpec(memory_space=pltpu.SMEM)
VMEM = pl.BlockSpec(memory_space=pltpu.VMEM)


def call(body, outs, args, scratch=(), scalar=False, alias=None):
    specs = [VMEM] * len(args)
    if scalar:
        specs[0] = SMEM
    return pl.pallas_call(
        body,
        out_shape=[jax.ShapeDtypeStruct(s, d) for s, d in outs],
        in_specs=specs,
        out_specs=[VMEM] * len(outs),
        scratch_shapes=list(scratch),
        input_output_aliases=alias or {},
        compiler_params=pltpu.CompilerParams(vmem_limit_bytes=VMEM_LIMIT),
    )(*args)


def after(value, *others):
    return lax.optimization_barrier((value,) + others)[0]


HALF = LANES


def band_of(products, dyi):
    lane = iota((8, HALF), 1)
    near = jnp.where(lane >= HALF - 8, products[HALF - 8:HALF, :HALF], products[HALF - 8:HALF, HALF:])
    far = jnp.where(lane < 8, products[HALF:HALF + 8, HALF:], products[HALF:HALF + 8, :HALF])
    ring = jnp.concatenate([products[:HALF - 8, HALF:], near, far, products[HALF + 8:, :HALF]], axis=0)
    band = pltpu.roll(ring, 8, 1, stride=1, stride_axis=0)
    return pltpu.roll(band, (9 * dyi - 3) % LANES, 1)


def spread_of(bands, dyi):
    moved = pltpu.roll(bands, (4 - 9 * dyi) % LANES, 1)
    lane = iota(bands.shape, 1)
    own = jnp.where((lane >= 4) & (lane < 13), moved, 0.0)
    ring = pltpu.roll(own, HALF - 8, 1, stride=1, stride_axis=0)
    edge = iota((8, HALF), 1)
    none = jnp.zeros((8, HALF), f32)
    near = ring[HALF - 8:HALF]
    far = ring[HALF:HALF + 8]
    left = jnp.concatenate([ring[HALF - 16:HALF - 8], jnp.where(edge < 8, 0.0, near), jnp.where(edge >= HALF - 8, far, 0.0), none], axis=0)
    right = jnp.concatenate([none, jnp.where(edge < 8, near, 0.0), jnp.where(edge >= HALF - 8, 0.0, far), ring[HALF + 8:HALF + 16]], axis=0)
    zero = jnp.zeros((HALF - 16, HALF), bf16)
    left = jnp.concatenate([ring[:HALF - 16].astype(bf16), left.astype(bf16), zero], axis=0)
    right = jnp.concatenate([zero, right.astype(bf16), ring[HALF + 16:].astype(bf16)], axis=0)
    return jnp.concatenate([left, right], axis=1)


def lane_valid(rows):
    lane = iota((rows, LANES), 1)
    col = iota((rows, LANES), 0) + lane % WIN - RADIUS
    return (col >= 0) & (col < rows) & (lane < K)


def corr_rows(first_ref, second_ref, start, before, put):
    rows, cols = first_ref.shape[0], first_ref.shape[1]
    count = second_ref.shape[0]
    lane = iota((cols, LANES), 1)
    valid = lane_valid(cols)
    mirror = (iota((cols, cols), 0) + iota((cols, cols), 1) == cols - 1).astype(bf16)
    for r in range(rows):
        dys = [q - r + RADIUS for q in range(start, start + count) if abs(q - r) <= RADIUS]
        if not dys:
            put(r, before[r])
            continue
        turned = dot(mirror, first_ref[r]).astype(bf16)
        acc = jnp.zeros((cols, LANES), f32)
        for dyi in dys:
            band = band_of(dot(turned, second_ref[r + dyi - RADIUS - start], NT), dyi)
            acc = jnp.where((lane >= 9 * dyi) & (lane < 9 * dyi + 9), band, acc)
        acc = jnp.where(valid, dot(mirror, (acc * (C ** -0.5)).astype(bf16)), 0.0)
        if before is None:
            acc = jnp.where(lane == K, 1.0, acc)
        else:
            inside = (lane >= 9 * dys[0]) & (lane < 9 * dys[-1] + 9)
            acc = jnp.where(inside, acc, before[r].astype(f32))
        put(r, acc.astype(bf16))


def corr_own_body(first_ref, own_ref, corr_ref):
    corr_rows(first_ref, own_ref, 0, None, lambda r, v: corr_ref.__setitem__(r, v))


def corr_halo_body(par_ref, first_ref, old_ref, low_ref, high_ref, corr_ref, ea_ref, eb_ref, mid_ref):
    rows = first_ref.shape[0]
    par = par_ref[0] & 1
    corr_rows(first_ref, low_ref, -low_ref.shape[0], old_ref, lambda r, v: mid_ref.__setitem__(r, v))
    corr_rows(first_ref, high_ref, rows, mid_ref, lambda r, v: corr_ref.__setitem__(r, v))
    ea_ref[...] = corr_ref[(1 - par) * (rows - 1)]
    eb_ref[...] = corr_ref[par * (rows - 1)]


def shift_down(x, steps):
    zero = jnp.zeros((abs(steps), x.shape[1]), x.dtype)
    if steps > 0:
        return jnp.concatenate([zero, x[:-steps]], axis=0)
    return jnp.concatenate([x[-steps:], zero], axis=0)


def put_taps(x_ref, slot, value):
    wide = value.astype(f32)
    x_ref[slot, :, 0:LANES] = shift_down(wide, 1).astype(bf16)
    x_ref[slot, :, LANES:2 * LANES] = value
    x_ref[slot, :, 2 * LANES:] = shift_down(wide, -1).astype(bf16)


def cell_row(pre, r, head, target_ref, mask_ref):
    cols = pre.shape[0]
    sig = lax.logistic(pre)
    hidden = (pre * sig).astype(bf16)
    pred = dot(head, hidden, NT)
    err = mask_ref[r:r + 1, :] * (pred[0:2] - target_ref[:, r, :])
    err = jnp.concatenate([err, jnp.zeros((head.shape[0] - 2, cols), f32)], axis=0).astype(bf16)
    herr = dot(err, head, TN)
    pe = (herr * sig * (1.0 + pre * (1.0 - sig))).astype(bf16)
    return pe, dot(err, hidden)


def conv_own_body(corr_ref, w_ref, bias_ref, head_ref, target_ref, mask_ref, x_ref, pre_ref, pe_ref, part_ref, hsum_ref, pt_ref):
    rows, cols = corr_ref.shape[0], corr_ref.shape[1]
    for r in range(rows):
        put_taps(x_ref, r, corr_ref[r])
    head = head_ref[...]
    pre_ref[0] = bias_ref[...] + (dot(x_ref[0], w_ref[1]) + dot(x_ref[1], w_ref[2]))
    pre_ref[1] = bias_ref[...] + (dot(x_ref[rows - 2], w_ref[0]) + dot(x_ref[rows - 1], w_ref[1]))
    total = jnp.zeros(hsum_ref.shape, f32)
    for r in range(1, rows - 1):
        pre = bias_ref[...] + (dot(x_ref[r - 1], w_ref[0]) + dot(x_ref[r], w_ref[1]) + dot(x_ref[r + 1], w_ref[2]))
        pe, head_sum = cell_row(pre, r, head, target_ref, mask_ref)
        total = total + head_sum
        pe_ref[r - 1] = pe
        pt_ref[:, (r - 1) * cols:r * cols] = pe.T
    hsum_ref[...] = total
    for ty in range(3):
        x = x_ref[ty:ty + rows - 2].reshape((rows - 2) * cols, 3 * LANES)
        part_ref[:, ty * 3 * LANES:(ty + 1) * 3 * LANES] = dot(pt_ref[...], x)


def conv_edge_body(par_ref, x_ref, pre_ref, part_ref, hsum_ref, ha_ref, hb_ref, w_ref, head_ref, target_ref, mask_ref,
                   pe_ref, pa_ref, pb_ref, keep_ref, send_ref, h_ref, pt_ref):
    rows, cols = x_ref.shape[0], x_ref.shape[1]
    hid = w_ref.shape[2]
    par = par_ref[0] & 1
    put_taps(h_ref, 1 - par, ha_ref[...])
    put_taps(h_ref, par, hb_ref[...])
    head = head_ref[...]
    head_sum = hsum_ref[...]
    for i, r in enumerate((0, rows - 1)):
        pre = pre_ref[i] + dot(h_ref[i], w_ref[2 * i])
        pe, own_sum = cell_row(pre, r, head, target_ref, mask_ref)
        head_sum = head_sum + own_sum
        pe_ref[i] = pe
        pt_ref[i] = pe.T
    pa_ref[...] = pe_ref[1 - par]
    pb_ref[...] = pe_ref[par]
    top, bottom = pt_ref[0], pt_ref[1]
    pieces = []
    bias_col = None
    for ty in range(3):
        low = h_ref[0] if ty == 0 else x_ref[ty - 1]
        high = h_ref[1] if ty == 2 else x_ref[rows - 2 + ty]
        part = part_ref[:, ty * 3 * LANES:(ty + 1) * 3 * LANES] + (dot(top, low) + dot(bottom, high))
        for tx in range(3):
            pieces.append(part[:, tx * LANES:tx * LANES + K])
        if ty == 1:
            bias_col = part[:, LANES + K:LANES + K + 1]
    head_cols = jnp.concatenate([head_sum, jnp.zeros((LANES - head.shape[0], hid), f32)], axis=0).T
    pad = jnp.zeros((hid, WIDTH - 9 * K - 3), f32)
    sums = jnp.concatenate(pieces + [bias_col, head_cols[:, 0:2], pad], axis=1)
    upper, lower = sums[:hid // 2], sums[hid // 2:]
    keep_ref[...] = jnp.where(par == 0, upper, lower)
    send_ref[...] = jnp.where(par == 0, lower, upper)


def halve_body(index_ref, own_ref, got_ref, keep_ref, send_ref, *, step):
    half = keep_ref.shape[0]
    bit = (index_ref[0] >> step) & 1
    upper = own_ref[:half] + got_ref[:half]
    lower = own_ref[half:] + got_ref[half:]
    keep_ref[...] = jnp.where(bit == 0, upper, lower)
    send_ref[...] = jnp.where(bit == 0, lower, upper)


def add_body(own_ref, got_ref, out_ref):
    out_ref[...] = own_ref[...] + got_ref[...]


def tail_body(own_ref, got_ref, conv_ref, rest_ref, square_ref):
    piece = own_ref[...] + got_ref[...]
    share = piece.shape[0]
    for tap in range(9):
        conv_ref[tap] = piece[:, tap * K:(tap + 1) * K]
    start = 9 * K // LANES * LANES
    rest = jnp.concatenate([piece[:, start:start + LANES], jnp.zeros((LANES - share, LANES), f32)], axis=0)
    rest_ref[...] = rest.T[9 * K - start:9 * K - start + 3, 0:share]
    square_ref[...] = jnp.broadcast_to(jnp.sum(piece * piece).reshape(1, 1), square_ref.shape)


def final_body(sq_ref, got_ref, conv_ref, rest_ref, out_ref, bias_ref, head_ref, *, limit):
    factor = jnp.minimum(1.0, limit / jnp.sqrt(sq_ref[0:1, 0:1] + got_ref[0:1, 0:1] + 1e-06))
    out_ref[...] = conv_ref[...] * factor.reshape(1, 1, 1)
    bias_ref[...] = rest_ref[0:1] * factor
    head_ref[...] = rest_ref[1:3] * factor


def cerr_row(z0, z1, z2):
    z = z0 + z1 + z2
    return shift_down(z[:, 0:LANES], -1) + z[:, LANES:2 * LANES] + shift_down(z[:, 2 * LANES:], 1)


def cerr_own_body(mid_ref, edge_ref, w_ref, ce_ref, rest_ref):
    rows = mid_ref.shape[0] + 2
    cols = mid_ref.shape[1]
    valid = lane_valid(cols)
    row = lambda r: edge_ref[0] if r == 0 else (edge_ref[1] if r == rows - 1 else mid_ref[r - 1])
    for r in range(rows):
        parts = [dot(row(r + 1 - ty), w_ref[ty], NT) for ty in range(3) if 0 <= r + 1 - ty < rows]
        total = cerr_row(parts[0], parts[1], parts[2] if len(parts) == 3 else 0.0)
        if 0 < r < rows - 1:
            ce_ref[r - 1] = jnp.where(valid, total * (C ** -0.5), 0.0).astype(bf16)
        else:
            rest_ref[min(r, 1)] = total


def cerr_edge_body(par_ref, mid_ref, rest_ref, ha_ref, hb_ref, w_ref, ce_ref, ea_ref, eb_ref, h_ref):
    rows = mid_ref.shape[0] + 2
    cols = mid_ref.shape[1]
    par = par_ref[0] & 1
    h_ref[1 - par] = ha_ref[...]
    h_ref[par] = hb_ref[...]
    valid = lane_valid(cols)
    lane = iota((cols, LANES), 1)
    for i in range(2):
        total = rest_ref[i] + cerr_row(dot(h_ref[i], w_ref[2 - 2 * i], NT), 0.0, 0.0)
        ce_ref[i] = jnp.where(valid, total * (C ** -0.5), 0.0).astype(bf16)
    to_low = jnp.zeros((cols, LANES), f32)
    to_high = jnp.zeros((cols, LANES), f32)
    low_at = high_at = 0
    for r in range(rows):
        total = (ce_ref[min(r, 1)] if r in (0, rows - 1) else mid_ref[r - 1]).astype(f32)
        count = 9 * (RADIUS - r)
        moved = pltpu.roll(total, low_at, 1) if low_at else total
        to_low = jnp.where((lane >= low_at) & (lane < low_at + count), moved, to_low)
        low_at += count
        count = 9 * (r + 1 + RADIUS - rows)
        start = K - count
        moved = pltpu.roll(total, (high_at - start) % LANES, 1)
        to_high = jnp.where((lane >= high_at) & (lane < high_at + count), moved, to_high)
        high_at += count
    up = to_low.astype(bf16)
    down = to_high.astype(bf16)

    @pl.when(par == 0)
    def _():
        ea_ref[...] = down
        eb_ref[...] = up

    @pl.when(par != 0)
    def _():
        ea_ref[...] = up
        eb_ref[...] = down


def row_grad_body(ce_ref, first_ref, second_ref, low_ref, high_ref, *refs, r, at, done):
    fg_ref, part_ref = refs[-2:]
    old_ref = refs[0] if len(refs) > 2 else None
    rows, cols = first_ref.shape[0], first_ref.shape[1]
    bands = ce_ref[at].astype(f32)
    turned = first_ref[r].T
    acc = jnp.zeros((cols, C), f32)
    for dyi in range(WIN):
        q = r + dyi - RADIUS
        src = low_ref[q + RADIUS] if q < 0 else (high_ref[q - rows] if q >= rows else second_ref[q])
        spread = spread_of(bands, dyi)
        acc = acc + dot(spread, src)
        if 0 <= q < rows:
            gave = dot(turned, spread)
            part_ref[q] = gave if old_ref is None else old_ref[q] + gave
    fg_ref[r if done else 0] = acc.astype(bf16)
    for other, row_ref in zip(done, refs[1:]):
        fg_ref[other] = row_ref[0]


def halo_part(bands, rows_ref, dys_of, old_ref):
    rows = old_ref.shape[0]
    parts = [old_ref[q] for q in range(rows)]
    slot = 0
    for r in range(rows):
        turned = rows_ref[r].T
        for q in dys_of(r):
            parts[q] = parts[q] + dot(turned, spread_of(bands, slot))
            slot += 1
    return parts


def halo_above_body(index_ref, ca_ref, cb_ref, low_ref, old_ref, part_ref):
    par = index_ref[0] & 1
    rows = part_ref.shape[0]
    bands = jnp.where(par == 0, cb_ref[...].astype(f32), ca_ref[...].astype(f32))
    parts = halo_part(bands, low_ref, lambda a: range(0, a + RADIUS + 1 - rows), old_ref)
    for q in range(rows):
        part_ref[q] = parts[q]


def halo_below_body(index_ref, ca_ref, cb_ref, high_ref, part_ref, sg_ref):
    par = index_ref[0] & 1
    rows = part_ref.shape[0]
    bands = jnp.where(par == 0, ca_ref[...].astype(f32), cb_ref[...].astype(f32))
    parts = halo_part(bands, high_ref, lambda b: range(rows + b - RADIUS, rows), part_ref)
    for q in range(rows):
        sg_ref[q] = parts[q].T.astype(bf16)


def on_device(first_map, second_map, flow_target, valid_tiles, conv_weight, conv_bias, head_weight):
    rows, cols = first_map.shape[0], first_map.shape[1]
    hid = conv_weight.shape[2]
    count = lax.axis_size("region")
    index = lax.axis_index("region")
    par = index.reshape(1)
    forward = [(i, i + 1) for i in range(count - 1)]
    backward = [(b, a) for a, b in forward]
    inner = [(i, i ^ 1) for i in range(count)]
    outer = [(i, i + 1) for i in range(1, count - 1, 2)]
    outer = outer + [(b, a) for a, b in outer]

    def permute(x, pairs):
        return lax.ppermute(x, "region", pairs)

    def swap(x, step):
        return permute(x, [(i, i ^ (1 << step)) for i in range(count)])

    second_low = permute(second_map, forward)
    second_high = permute(second_map, backward)

    share = hid // count
    radix = [2] * (count.bit_length() - 1)
    turn = tuple(reversed(range(len(radix)))) + (len(radix),)

    def reorder(x):
        return jnp.transpose(x.reshape(tuple(radix) + (share,)), turn).reshape(hid)

    order = reorder(jnp.arange(hid))
    select = (jnp.arange(hid)[:, None] == order[None, :]).astype(bf16)
    weight = jnp.einsum("tkh,hg->tkg", conv_weight, select, preferred_element_type=bf16)
    weight = jnp.pad(weight, ((0, 0), (0, LANES - K), (0, 0))).reshape(3, 3 * LANES, hid)
    head = jnp.einsum("jh,hg->jg", head_weight, select, preferred_element_type=bf16)
    head = jnp.pad(head, ((0, 14), (0, 0)))
    bias = reorder(conv_bias).reshape(1, hid)
    tile_rows = jnp.repeat(valid_tiles, TILE, axis=0)
    own_tiles = lax.dynamic_slice_in_dim(tile_rows, index * rows, rows, 0)
    mask = jnp.repeat(own_tiles, TILE, axis=1).astype(f32)

    vector = lambda *s: pltpu.VMEM(s, bf16)
    (corr_own,) = call(corr_own_body, [((rows, cols, LANES), bf16)], (first_map, second_map))
    weight, head, bias, mask, corr_own, second_low, second_high = lax.optimization_barrier(
        (weight, head, bias, mask, corr_own, second_low, second_high)
    )
    corr, edge_a, edge_b = call(
        corr_halo_body,
        [((rows, cols, LANES), bf16), ((cols, LANES), bf16), ((cols, LANES), bf16)],
        (par, first_map, corr_own, second_low, second_high),
        scratch=[vector(rows, cols, LANES)],
        scalar=True,
    )
    halo_a = permute(edge_a, inner)
    halo_b = permute(edge_b, outer)
    taps, pre_edge, pe_mid, part_sums, head_part = call(
        conv_own_body,
        [((rows, cols, 3 * LANES), bf16), ((2, cols, hid), f32), ((rows - 2, cols, hid), bf16), ((hid, 9 * LANES), f32), ((16, hid), f32)],
        (corr, weight, bias, head, flow_target, mask),
        scratch=[vector(hid, (rows - 2) * cols)],
    )
    halo_a, halo_b, taps = lax.optimization_barrier((halo_a, halo_b, taps))
    pe_edge, pe_a, pe_b, keep, send = call(
        conv_edge_body,
        [((2, cols, hid), bf16), ((cols, hid), bf16), ((cols, hid), bf16), ((hid // 2, WIDTH), f32), ((hid // 2, WIDTH), f32)],
        (par, taps, pre_edge, part_sums, head_part, halo_a, halo_b, weight, head, flow_target, mask),
        scratch=[vector(2, cols, 3 * LANES), vector(2, hid, cols)],
        scalar=True,
    )
    got = swap(send, 0)
    pe_halo_a = permute(pe_a, inner)
    pe_halo_b = permute(pe_b, outer)

    def halve(step, keep, got):
        half = keep.shape[0] // 2
        return call(functools.partial(halve_body, step=step), [((half, WIDTH), f32)] * 2, (par, keep, got), scalar=True)

    def row_grad(r, at, cerr, part, done=()):
        args = (cerr, first_map, second_map, second_low, second_high)
        if part is not None:
            args = args + (part,) + tuple(row for _, row in done)
        return call(
            functools.partial(row_grad_body, r=r, at=at, done=[other for other, _ in done]),
            [((rows if done else 1, cols, C), bf16), ((rows, C, cols), f32)],
            args,
            alias=None if part is None else {5: 1},
        )

    steps = len(radix)
    keep, send = halve(1, keep, got)
    got = swap(send, 1)
    ce_mid, ce_rest = call(
        cerr_own_body,
        [((rows - 2, cols, LANES), bf16), ((2, cols, LANES), f32)],
        (after(pe_mid, send), pe_edge, weight),
    )
    part = None
    done = []
    for r in range(1, rows - 1):
        row, part = row_grad(r, r - 1, ce_mid, part)
        done.append((r, row))
    got, part = lax.optimization_barrier((got, part))
    keep, send = halve(2, keep, got)
    got = swap(send, 2)
    ce_edge, ce_a, ce_b = call(
        cerr_edge_body,
        [((2, cols, LANES), bf16), ((cols, LANES), bf16), ((cols, LANES), bf16)],
        (par, ce_mid, after(ce_rest, send), pe_halo_a, pe_halo_b, weight),
        scratch=[vector(2, cols, hid)],
        scalar=True,
    )
    ce_halo_a = permute(ce_a, inner)
    ce_halo_b = permute(ce_b, outer)
    first_tied = after(first_map, ce_a)
    first_low = permute(first_tied, forward)
    first_high = permute(first_tied, backward)
    row, part = row_grad(0, 0, ce_edge, part)
    done.append((0, row))
    got, part = lax.optimization_barrier((got, part))
    for step in range(3, steps):
        keep, send = halve(step, keep, got)
        got = swap(send, step)
    first_grad, part = row_grad(rows - 1, 1, after(ce_edge, send), part, done)
    got, part, ce_halo_a, ce_halo_b = lax.optimization_barrier((got, part, ce_halo_a, ce_halo_b))
    conv_raw, rest_raw, square = call(
        tail_body,
        [((9, share, K), f32), ((3, share), f32), ((8, LANES), f32)],
        (keep, got),
    )

    def add(x, y):
        return call(add_body, [((8, LANES), f32)], (x, y))[0]

    got = swap(square, 0)
    square = add(square, got)
    got = swap(square, 1)
    (part,) = call(
        halo_above_body,
        [((rows, C, cols), f32)],
        (par, after(ce_halo_a, square), ce_halo_b, first_low, part),
        scalar=True,
        alias={4: 0},
    )
    got, part = lax.optimization_barrier((got, part))
    square = add(square, got)
    got = swap(square, 2)
    (second_grad,) = call(
        halo_below_body,
        [((rows, cols, C), bf16)],
        (par, after(ce_halo_a, square), ce_halo_b, first_high, part),
        scalar=True,
    )
    got, second_grad = lax.optimization_barrier((got, second_grad))
    for step in range(3, steps):
        square = add(square, got)
        got = swap(square, step)
    param_count = 9 * K * hid + 3 * hid
    conv_piece, bias_piece, head_piece = call(
        functools.partial(final_body, limit=clip_fraction * param_count ** 0.5),
        [((9, share, K), f32), ((1, share), f32), ((2, share), f32)],
        (square, got, conv_raw, rest_raw),
    )
    return first_grad, second_grad, jnp.transpose(conv_piece, (0, 2, 1)), bias_piece.reshape(share), head_piece


def solution(mesh):
    return jax.shard_map(
        on_device,
        mesh=mesh,
        in_specs=(
            P("region", "group", None),
            P("region", "group", None),
            P(None, "region", "group"),
            P(None, "group"),
            P(),
            P(),
            P(),
        ),
        out_specs=(
            P("region", "group", None),
            P("region", "group", None),
            P("group", None, "region"),
            P(("group", "region")),
            P("group", "region"),
        ),
        check_vma=False,
    )
```

```python
import functools

import jax
import jax.numpy as jnp
from jax import lax
from jax.experimental import pallas as pl
from jax.experimental.pallas import tpu as pltpu
from jax.sharding import PartitionSpec as P

C = 256
RADIUS = 4
TILE = 16
K = 81
WIN = 9
LANES = 128

clip_fraction = 0.25
WIDTH = 768
VMEM_LIMIT = 24 * 1024 * 1024

f32 = jnp.float32
bf16 = jnp.bfloat16

NT = (((1,), (1,)), ((), ()))
TN = (((0,), (0,)), ((), ()))


def dot(a, b, dims=None):
    if dims is None:
        return jnp.dot(a, b, preferred_element_type=f32)
    return lax.dot_general(a, b, dims, preferred_element_type=f32)


def iota(shape, dim):
    return lax.broadcasted_iota(jnp.int32, shape, dim)


SMEM = pl.BlockSpec(memory_space=pltpu.SMEM)
VMEM = pl.BlockSpec(memory_space=pltpu.VMEM)


def call(body, outs, args, scratch=(), scalar=False, alias=None):
    specs = [VMEM] * len(args)
    if scalar:
        specs[0] = SMEM
    return pl.pallas_call(
        body,
        out_shape=[jax.ShapeDtypeStruct(s, d) for s, d in outs],
        in_specs=specs,
        out_specs=[VMEM] * len(outs),
        scratch_shapes=list(scratch),
        input_output_aliases=alias or {},
        compiler_params=pltpu.CompilerParams(vmem_limit_bytes=VMEM_LIMIT),
    )(*args)


def after(value, *others):
    return lax.optimization_barrier((value,) + others)[0]


HALF = LANES


def band_of(products, dyi):
    lane = iota((8, HALF), 1)
    near = jnp.where(lane >= HALF - 8, products[HALF - 8:HALF, :HALF], products[HALF - 8:HALF, HALF:])
    far = jnp.where(lane < 8, products[HALF:HALF + 8, HALF:], products[HALF:HALF + 8, :HALF])
    ring = jnp.concatenate([products[:HALF - 8, HALF:], near, far, products[HALF + 8:, :HALF]], axis=0)
    band = pltpu.roll(ring, 8, 1, stride=1, stride_axis=0)
    return pltpu.roll(band, (9 * dyi - 3) % LANES, 1)


def spread_of(bands, dyi):
    moved = pltpu.roll(bands, (4 - 9 * dyi) % LANES, 1)
    lane = iota(bands.shape, 1)
    own = jnp.where((lane >= 4) & (lane < 13), moved, 0.0)
    ring = pltpu.roll(own, HALF - 8, 1, stride=1, stride_axis=0)
    edge = iota((8, HALF), 1)
    none = jnp.zeros((8, HALF), f32)
    near = ring[HALF - 8:HALF]
    far = ring[HALF:HALF + 8]
    left = jnp.concatenate([ring[HALF - 16:HALF - 8], jnp.where(edge < 8, 0.0, near), jnp.where(edge >= HALF - 8, far, 0.0), none], axis=0)
    right = jnp.concatenate([none, jnp.where(edge < 8, near, 0.0), jnp.where(edge >= HALF - 8, 0.0, far), ring[HALF + 8:HALF + 16]], axis=0)
    zero = jnp.zeros((HALF - 16, HALF), bf16)
    left = jnp.concatenate([ring[:HALF - 16].astype(bf16), left.astype(bf16), zero], axis=0)
    right = jnp.concatenate([zero, right.astype(bf16), ring[HALF + 16:].astype(bf16)], axis=0)
    return jnp.concatenate([left, right], axis=1)


def lane_valid(rows):
    lane = iota((rows, LANES), 1)
    col = iota((rows, LANES), 0) + lane % WIN - RADIUS
    return (col >= 0) & (col < rows) & (lane < K)


def corr_rows(turned_ref, second_ref, start, before, put):
    rows, cols = turned_ref.shape[0], turned_ref.shape[1]
    count = second_ref.shape[0]
    lane = iota((cols, LANES), 1)
    valid = lane_valid(cols)
    mirror = mirror_of(cols)
    for r in range(rows):
        dys = [q - r + RADIUS for q in range(start, start + count) if abs(q - r) <= RADIUS]
        if not dys:
            put(r, before[r])
            continue
        acc = jnp.zeros((cols, LANES), f32)
        for dyi in dys:
            band = band_of(dot(turned_ref[r], second_ref[r + dyi - RADIUS - start], NT), dyi)
            acc = jnp.where((lane >= 9 * dyi) & (lane < 9 * dyi + 9), band, acc)
        acc = jnp.where(valid, dot(mirror, (acc * (C ** -0.5)).astype(bf16)), 0.0)
        if before is None:
            acc = jnp.where(lane == K, 1.0, acc)
        else:
            inside = (lane >= 9 * dys[0]) & (lane < 9 * dys[-1] + 9)
            acc = jnp.where(inside, acc, before[r].astype(f32))
        put(r, acc.astype(bf16))


def mirror_of(cols):
    return (iota((cols, cols), 0) + iota((cols, cols), 1) == cols - 1).astype(bf16)


def by_side(below, body):
    pl.when(below)(lambda: body(True))
    pl.when(jnp.logical_not(below))(lambda: body(False))


def corr_near_body(index_ref, first_ref, own_ref, inner_ref, corr_ref, turned_ref, mid_ref):
    rows, cols = first_ref.shape[0], first_ref.shape[1]
    mirror = mirror_of(cols)
    for r in range(rows):
        turned_ref[r] = dot(mirror, first_ref[r]).astype(bf16)
    corr_rows(turned_ref, own_ref, 0, None, lambda r, v: mid_ref.__setitem__(r, v))

    def side(below):
        corr_rows(turned_ref, inner_ref, rows if below else -rows, mid_ref, lambda r, v: corr_ref.__setitem__(r, v))

    by_side(index_ref[0] & 1 == 0, side)


def corr_outer_body(index_ref, turned_ref, old_ref, outer_ref, corr_ref, ea_ref, eb_ref):
    rows = turned_ref.shape[0]
    par = index_ref[0] & 1

    def side(below):
        corr_rows(turned_ref, outer_ref, rows if below else -rows, old_ref, lambda r, v: corr_ref.__setitem__(r, v))
        ea_ref[...] = corr_ref[0 if below else rows - 1]
        eb_ref[...] = corr_ref[rows - 1 if below else 0]

    by_side(par == 1, side)


def shift_down(x, steps):
    zero = jnp.zeros((abs(steps), x.shape[1]), x.dtype)
    if steps > 0:
        return jnp.concatenate([zero, x[:-steps]], axis=0)
    return jnp.concatenate([x[-steps:], zero], axis=0)


def put_taps(x_ref, slot, value):
    wide = value.astype(f32)
    x_ref[slot, :, 0:LANES] = shift_down(wide, 1).astype(bf16)
    x_ref[slot, :, LANES:2 * LANES] = value
    x_ref[slot, :, 2 * LANES:] = shift_down(wide, -1).astype(bf16)


def cell_row(pre, r, head, target_ref, mask_ref):
    cols = pre.shape[0]
    sig = lax.logistic(pre)
    hidden = (pre * sig).astype(bf16)
    pred = dot(head, hidden, NT)
    err = mask_ref[r:r + 1, :] * (pred[0:2] - target_ref[:, r, :])
    err = jnp.concatenate([err, jnp.zeros((head.shape[0] - 2, cols), f32)], axis=0).astype(bf16)
    herr = dot(err, head, TN)
    pe = (herr * sig * (1.0 + pre * (1.0 - sig))).astype(bf16)
    return pe, dot(err, hidden)


def conv_own_body(corr_ref, w_ref, bias_ref, head_ref, target_ref, mask_ref, x_ref, pre_ref, pe_ref, part_ref, hsum_ref, pt_ref):
    rows, cols = corr_ref.shape[0], corr_ref.shape[1]
    for r in range(rows):
        put_taps(x_ref, r, corr_ref[r])
    head = head_ref[...]
    pre_ref[0] = bias_ref[...] + (dot(x_ref[0], w_ref[1]) + dot(x_ref[1], w_ref[2]))
    pre_ref[1] = bias_ref[...] + (dot(x_ref[rows - 2], w_ref[0]) + dot(x_ref[rows - 1], w_ref[1]))
    total = jnp.zeros(hsum_ref.shape, f32)
    for r in range(1, rows - 1):
        pre = bias_ref[...] + (dot(x_ref[r - 1], w_ref[0]) + dot(x_ref[r], w_ref[1]) + dot(x_ref[r + 1], w_ref[2]))
        pe, head_sum = cell_row(pre, r, head, target_ref, mask_ref)
        total = total + head_sum
        pe_ref[r - 1] = pe
        pt_ref[:, (r - 1) * cols:r * cols] = pe.T
    hsum_ref[...] = total
    for ty in range(3):
        x = x_ref[ty:ty + rows - 2].reshape((rows - 2) * cols, 3 * LANES)
        part_ref[:, ty * 3 * LANES:(ty + 1) * 3 * LANES] = dot(pt_ref[...], x)


def conv_edge_body(par_ref, x_ref, pre_ref, part_ref, hsum_ref, ha_ref, hb_ref, w_ref, head_ref, target_ref, mask_ref,
                   pe_ref, pa_ref, pb_ref, keep_ref, send_ref, h_ref, pt_ref):
    rows, cols = x_ref.shape[0], x_ref.shape[1]
    hid = w_ref.shape[2]
    par = par_ref[0] & 1
    put_taps(h_ref, 1 - par, ha_ref[...])
    put_taps(h_ref, par, hb_ref[...])
    head = head_ref[...]
    head_sum = hsum_ref[...]
    for i, r in enumerate((0, rows - 1)):
        pre = pre_ref[i] + dot(h_ref[i], w_ref[2 * i])
        pe, own_sum = cell_row(pre, r, head, target_ref, mask_ref)
        head_sum = head_sum + own_sum
        pe_ref[i] = pe
        pt_ref[i] = pe.T
    pa_ref[...] = pe_ref[1 - par]
    pb_ref[...] = pe_ref[par]
    top, bottom = pt_ref[0], pt_ref[1]
    pieces = []
    bias_col = None
    for ty in range(3):
        low = h_ref[0] if ty == 0 else x_ref[ty - 1]
        high = h_ref[1] if ty == 2 else x_ref[rows - 2 + ty]
        part = part_ref[:, ty * 3 * LANES:(ty + 1) * 3 * LANES] + (dot(top, low) + dot(bottom, high))
        for tx in range(3):
            pieces.append(part[:, tx * LANES:tx * LANES + K])
        if ty == 1:
            bias_col = part[:, LANES + K:LANES + K + 1]
    head_cols = jnp.concatenate([head_sum, jnp.zeros((LANES - head.shape[0], hid), f32)], axis=0).T
    pad = jnp.zeros((hid, WIDTH - 9 * K - 3), f32)
    sums = jnp.concatenate(pieces + [bias_col, head_cols[:, 0:2], pad], axis=1)
    upper, lower = sums[:hid // 2], sums[hid // 2:]
    keep_ref[...] = jnp.where(par == 0, upper, lower)
    send_ref[...] = jnp.where(par == 0, lower, upper)


def halve_body(index_ref, own_ref, got_ref, keep_ref, send_ref, *, step):
    half = keep_ref.shape[0]
    bit = (index_ref[0] >> step) & 1
    upper = own_ref[:half] + got_ref[:half]
    lower = own_ref[half:] + got_ref[half:]
    keep_ref[...] = jnp.where(bit == 0, upper, lower)
    send_ref[...] = jnp.where(bit == 0, lower, upper)


def add_body(own_ref, got_ref, out_ref):
    out_ref[...] = own_ref[...] + got_ref[...]


def tail_body(index_ref, own_ref, got_ref, conv_ref, rest_ref, square_ref, *, step):
    both = own_ref[...] + got_ref[...]
    share = conv_ref.shape[1]
    piece = jnp.where((index_ref[0] >> step) & 1 == 0, both[:share], both[share:])
    for tap in range(9):
        conv_ref[tap] = piece[:, tap * K:(tap + 1) * K]
    start = 9 * K // LANES * LANES
    rest = jnp.concatenate([piece[:, start:start + LANES], jnp.zeros((LANES - share, LANES), f32)], axis=0)
    rest_ref[...] = rest.T[9 * K - start:9 * K - start + 3, 0:share]
    square_ref[...] = jnp.broadcast_to(jnp.sum(both * both).reshape(1, 1), square_ref.shape)


def final_body(sq_ref, got_ref, conv_ref, rest_ref, out_ref, bias_ref, head_ref, *, limit):
    factor = jnp.minimum(1.0, limit / jnp.sqrt(sq_ref[0:1, 0:1] + got_ref[0:1, 0:1] + 1e-06))
    out_ref[...] = conv_ref[...] * factor.reshape(1, 1, 1)
    bias_ref[...] = rest_ref[0:1] * factor
    head_ref[...] = rest_ref[1:3] * factor


def cerr_row(z0, z1, z2):
    z = z0 + z1 + z2
    return shift_down(z[:, 0:LANES], -1) + z[:, LANES:2 * LANES] + shift_down(z[:, 2 * LANES:], 1)


def cerr_own_body(mid_ref, edge_ref, w_ref, ce_ref, rest_ref):
    rows = mid_ref.shape[0] + 2
    cols = mid_ref.shape[1]
    valid = lane_valid(cols)
    row = lambda r: edge_ref[0] if r == 0 else (edge_ref[1] if r == rows - 1 else mid_ref[r - 1])
    for r in range(rows):
        parts = [dot(row(r + 1 - ty), w_ref[ty], NT) for ty in range(3) if 0 <= r + 1 - ty < rows]
        total = cerr_row(parts[0], parts[1], parts[2] if len(parts) == 3 else 0.0)
        if 0 < r < rows - 1:
            ce_ref[r - 1] = jnp.where(valid, total * (C ** -0.5), 0.0).astype(bf16)
        else:
            rest_ref[min(r, 1)] = total


def cerr_edge_body(par_ref, mid_ref, rest_ref, ha_ref, hb_ref, w_ref, ce_ref, ea_ref, eb_ref, h_ref):
    rows = mid_ref.shape[0] + 2
    cols = mid_ref.shape[1]
    par = par_ref[0] & 1
    h_ref[1 - par] = ha_ref[...]
    h_ref[par] = hb_ref[...]
    valid = lane_valid(cols)
    lane = iota((cols, LANES), 1)
    for i in range(2):
        total = rest_ref[i] + cerr_row(dot(h_ref[i], w_ref[2 - 2 * i], NT), 0.0, 0.0)
        ce_ref[i] = jnp.where(valid, total * (C ** -0.5), 0.0).astype(bf16)
    to_low = jnp.zeros((cols, LANES), f32)
    to_high = jnp.zeros((cols, LANES), f32)
    low_at = high_at = 0
    for r in range(rows):
        total = (ce_ref[min(r, 1)] if r in (0, rows - 1) else mid_ref[r - 1]).astype(f32)
        count = 9 * (RADIUS - r)
        moved = pltpu.roll(total, low_at, 1) if low_at else total
        to_low = jnp.where((lane >= low_at) & (lane < low_at + count), moved, to_low)
        low_at += count
        count = 9 * (r + 1 + RADIUS - rows)
        start = K - count
        moved = pltpu.roll(total, (high_at - start) % LANES, 1)
        to_high = jnp.where((lane >= high_at) & (lane < high_at + count), moved, to_high)
        high_at += count
    up = to_low.astype(bf16)
    down = to_high.astype(bf16)

    @pl.when(par == 0)
    def _():
        ea_ref[...] = down
        eb_ref[...] = up

    @pl.when(par != 0)
    def _():
        ea_ref[...] = up
        eb_ref[...] = down


def row_grad_body(index_ref, ce_ref, first_ref, second_ref, inner_ref, outer_ref, *refs, r, at, done):
    fg_ref, part_ref = refs[-2:]
    old_ref = refs[0] if len(refs) > 2 else None
    rows, cols = first_ref.shape[0], first_ref.shape[1]
    even = index_ref[0] & 1 == 0
    bands = ce_ref[at].astype(f32)
    turned = first_ref[r].T
    acc = jnp.zeros((cols, C), f32)
    for dyi in range(WIN):
        q = r + dyi - RADIUS
        if q < 0:
            src = jnp.where(even, outer_ref[q + rows], inner_ref[q + rows])
        elif q >= rows:
            src = jnp.where(even, inner_ref[q - rows], outer_ref[q - rows])
        else:
            src = second_ref[q]
        spread = spread_of(bands, dyi)
        acc = acc + dot(spread, src)
        if 0 <= q < rows:
            gave = dot(turned, spread)
            part_ref[q] = gave if old_ref is None else old_ref[q] + gave
    fg_ref[r if done else 0] = acc.astype(bf16)
    for other, row_ref in zip(done, refs[1:]):
        fg_ref[other] = row_ref[0]


def halo_parts(bands_ref, rows_ref, below, old_ref):
    rows = old_ref.shape[0]
    bands = bands_ref[...].astype(f32)
    parts = [old_ref[q] for q in range(rows)]
    slot = 0
    for r in range(rows):
        turned = rows_ref[r].T
        for q in range(rows + r - RADIUS, rows) if below else range(0, r + RADIUS + 1 - rows):
            parts[q] = parts[q] + dot(turned, spread_of(bands, slot))
            slot += 1
    return parts


def halo_inner_body(index_ref, bands_ref, rows_ref, old_ref, part_ref):
    def side(below):
        for q, part in enumerate(halo_parts(bands_ref, rows_ref, below, old_ref)):
            part_ref[q] = part

    by_side(index_ref[0] & 1 == 0, side)


def halo_outer_body(index_ref, bands_ref, rows_ref, old_ref, sg_ref):
    def side(below):
        for q, part in enumerate(halo_parts(bands_ref, rows_ref, below, old_ref)):
            sg_ref[q] = part.T.astype(bf16)

    by_side(index_ref[0] & 1 == 1, side)


def on_device(first_map, second_map, flow_target, valid_tiles, conv_weight, conv_bias, head_weight):
    rows, cols = first_map.shape[0], first_map.shape[1]
    hid = conv_weight.shape[2]
    count = lax.axis_size("region")
    index = lax.axis_index("region")
    par = index.reshape(1)
    inner = [(i, i ^ 1) for i in range(count)]
    outer = [(i, i + 1) for i in range(1, count - 1, 2)]
    outer = outer + [(b, a) for a, b in outer]

    def permute(x, pairs):
        return lax.ppermute(x, "region", pairs)

    def swap(x, step):
        return permute(x, [(i, i ^ (1 << step)) for i in range(count)])

    second_outer = permute(second_map, outer)
    second_inner = permute(second_map, inner)
    first_inner = permute(first_map, inner)

    share = hid // count
    radix = [2] * (count.bit_length() - 1)
    turn = tuple(reversed(range(len(radix)))) + (len(radix),)

    def reorder(x):
        return jnp.transpose(x.reshape(tuple(radix) + (share,)), turn).reshape(hid)

    order = reorder(jnp.arange(hid))
    select = (jnp.arange(hid)[:, None] == order[None, :]).astype(bf16)
    weight = jnp.einsum("tkh,hg->tkg", conv_weight, select, preferred_element_type=bf16)
    weight = jnp.pad(weight, ((0, 0), (0, LANES - K), (0, 0))).reshape(3, 3 * LANES, hid)
    head = jnp.einsum("jh,hg->jg", head_weight, select, preferred_element_type=bf16)
    head = jnp.pad(head, ((0, 14), (0, 0)))
    bias = reorder(conv_bias).reshape(1, hid)
    tile_rows = jnp.repeat(valid_tiles, TILE, axis=0)
    own_tiles = lax.dynamic_slice_in_dim(tile_rows, index * rows, rows, 0)
    mask = jnp.repeat(own_tiles, TILE, axis=1).astype(f32)

    vector = lambda *s: pltpu.VMEM(s, bf16)
    corr_near, turned = call(
        corr_near_body,
        [((rows, cols, LANES), bf16), ((rows, cols, C), bf16)],
        (par, first_map, second_map, second_inner),
        scratch=[vector(rows, cols, LANES)],
        scalar=True,
    )
    weight, head, bias, mask, corr_near, second_outer, first_inner = lax.optimization_barrier(
        (weight, head, bias, mask, corr_near, second_outer, first_inner)
    )
    corr, edge_a, edge_b = call(
        corr_outer_body,
        [((rows, cols, LANES), bf16), ((cols, LANES), bf16), ((cols, LANES), bf16)],
        (par, turned, corr_near, second_outer),
        scalar=True,
    )
    halo_b = permute(edge_b, outer)
    halo_a = permute(edge_a, inner)
    taps, pre_edge, pe_mid, part_sums, head_part = call(
        conv_own_body,
        [((rows, cols, 3 * LANES), bf16), ((2, cols, hid), f32), ((rows - 2, cols, hid), bf16), ((hid, 9 * LANES), f32), ((16, hid), f32)],
        (corr, weight, bias, head, flow_target, mask),
        scratch=[vector(hid, (rows - 2) * cols)],
    )
    halo_a, halo_b, taps = lax.optimization_barrier((halo_a, halo_b, taps))
    pe_edge, pe_a, pe_b, keep, send = call(
        conv_edge_body,
        [((2, cols, hid), bf16), ((cols, hid), bf16), ((cols, hid), bf16), ((hid // 2, WIDTH), f32), ((hid // 2, WIDTH), f32)],
        (par, taps, pre_edge, part_sums, head_part, halo_a, halo_b, weight, head, flow_target, mask),
        scratch=[vector(2, cols, 3 * LANES), vector(2, hid, cols)],
        scalar=True,
    )
    got = swap(send, 0)
    pe_halo_a = permute(pe_a, inner)
    pe_halo_b = permute(pe_b, outer)

    def add(x, y):
        return call(add_body, [(x.shape, f32)], (x, y))[0]

    def halve(step, keep, got):
        half = keep.shape[0] // 2
        return call(functools.partial(halve_body, step=step), [((half, WIDTH), f32)] * 2, (par, keep, got), scalar=True)

    def row_grad(r, at, cerr, part, done=()):
        args = (par, cerr, first_map, second_map, second_inner, second_outer)
        if part is not None:
            args = args + (part,) + tuple(row for _, row in done)
        return call(
            functools.partial(row_grad_body, r=r, at=at, done=[other for other, _ in done]),
            [((rows if done else 1, cols, C), bf16), ((rows, C, cols), f32)],
            args,
            scalar=True,
            alias=None if part is None else {6: 1},
        )

    steps = len(radix)
    keep, send = halve(1, keep, got)
    got = swap(send, 1)
    ce_mid, ce_rest = call(
        cerr_own_body,
        [((rows - 2, cols, LANES), bf16), ((2, cols, LANES), f32)],
        (after(pe_mid, send), pe_edge, weight),
    )
    part = None
    done = []
    for r in range(1, rows - 1):
        row, part = row_grad(r, r - 1, ce_mid, part)
        done.append((r, row))
    got, part = lax.optimization_barrier((got, part))
    keep, send = halve(2, keep, got)
    got = swap(send, 2)
    ce_edge, ce_a, ce_b = call(
        cerr_edge_body,
        [((2, cols, LANES), bf16), ((cols, LANES), bf16), ((cols, LANES), bf16)],
        (par, ce_mid, after(ce_rest, send), pe_halo_a, pe_halo_b, weight),
        scratch=[vector(2, cols, hid)],
        scalar=True,
    )
    ce_outer = permute(ce_b, outer)
    ce_inner = permute(ce_a, inner)
    first_outer = permute(after(first_map, ce_a), outer)
    row, part = row_grad(0, 0, ce_edge, part)
    done.append((0, row))
    got, part = lax.optimization_barrier((got, part))
    for step in range(3, steps - 1):
        keep, send = halve(step, keep, got)
        got = swap(send, step)
    piece = add(keep, got)
    got = swap(piece, steps - 1)
    first_grad, part = row_grad(rows - 1, 1, after(ce_edge, piece), part, done)
    got, part, ce_inner, ce_outer = lax.optimization_barrier((got, part, ce_inner, ce_outer))
    conv_raw, rest_raw, square = call(
        functools.partial(tail_body, step=steps - 1),
        [((9, share, K), f32), ((3, share), f32), ((8, LANES), f32)],
        (par, piece, got),
        scalar=True,
    )
    got = swap(square, 0)
    square = add(square, got)
    got = swap(square, 1)
    (part,) = call(
        halo_inner_body,
        [((rows, C, cols), f32)],
        (par, after(ce_inner, square), first_inner, part),
        scalar=True,
        alias={3: 0},
    )
    got, part = lax.optimization_barrier((got, part))
    square = add(square, got)
    got = swap(square, 2)
    (second_grad,) = call(
        halo_outer_body,
        [((rows, cols, C), bf16)],
        (par, after(ce_outer, square), first_outer, part),
        scalar=True,
    )
    got, second_grad = lax.optimization_barrier((got, second_grad))
    for step in range(3, steps - 1):
        square = add(square, got)
        got = swap(square, step)
    param_count = 9 * K * hid + 3 * hid
    conv_piece, bias_piece, head_piece = call(
        functools.partial(final_body, limit=clip_fraction * param_count ** 0.5),
        [((9, share, K), f32), ((1, share), f32), ((2, share), f32)],
        (square, got, conv_raw, rest_raw),
    )
    return first_grad, second_grad, jnp.transpose(conv_piece, (0, 2, 1)), bias_piece.reshape(share), head_piece


def solution(mesh):
    return jax.shard_map(
        on_device,
        mesh=mesh,
        in_specs=(
            P("region", "group", None),
            P("region", "group", None),
            P(None, "region", "group"),
            P(None, "group"),
            P(),
            P(),
            P(),
        ),
        out_specs=(
            P("region", "group", None),
            P("region", "group", None),
            P("group", None, "region"),
            P(("group", "region")),
            P("group", "region"),
        ),
        check_vma=False,
    )
```

```python
import functools

import jax
import jax.numpy as jnp
from jax import lax
from jax.experimental import pallas as pl
from jax.experimental.pallas import tpu as pltpu
from jax.sharding import PartitionSpec as P

C = 256
RADIUS = 4
TILE = 16
K = 81
WIN = 9
LANES = 128

clip_fraction = 0.25
WIDTH = 768
VMEM_LIMIT = 24 * 1024 * 1024

f32 = jnp.float32
bf16 = jnp.bfloat16

NT = (((1,), (1,)), ((), ()))
TN = (((0,), (0,)), ((), ()))


def dot(a, b, dims=None):
    if dims is None:
        return jnp.dot(a, b, preferred_element_type=f32)
    return lax.dot_general(a, b, dims, preferred_element_type=f32)


def iota(shape, dim):
    return lax.broadcasted_iota(jnp.int32, shape, dim)


SMEM = pl.BlockSpec(memory_space=pltpu.SMEM)
VMEM = pl.BlockSpec(memory_space=pltpu.VMEM)


def call(body, outs, args, scratch=(), scalar=False, alias=None):
    specs = [VMEM] * len(args)
    if scalar:
        specs[0] = SMEM
    return pl.pallas_call(
        body,
        out_shape=[jax.ShapeDtypeStruct(s, d) for s, d in outs],
        in_specs=specs,
        out_specs=[VMEM] * len(outs),
        scratch_shapes=list(scratch),
        input_output_aliases=alias or {},
        compiler_params=pltpu.CompilerParams(vmem_limit_bytes=VMEM_LIMIT),
    )(*args)


def after(value, *others):
    return lax.optimization_barrier((value,) + others)[0]


HALF = LANES


def band_of(products, dyi):
    lane = iota((8, HALF), 1)
    near = jnp.where(lane >= HALF - 8, products[HALF - 8:HALF, :HALF], products[HALF - 8:HALF, HALF:])
    far = jnp.where(lane < 8, products[HALF:HALF + 8, HALF:], products[HALF:HALF + 8, :HALF])
    ring = jnp.concatenate([products[:HALF - 8, HALF:], near, far, products[HALF + 8:, :HALF]], axis=0)
    band = pltpu.roll(ring, 8, 1, stride=1, stride_axis=0)
    return pltpu.roll(band, (9 * dyi - 3) % LANES, 1)


def spread_of(bands, dyi):
    moved = pltpu.roll(bands, (4 - 9 * dyi) % LANES, 1)
    lane = iota(bands.shape, 1)
    own = jnp.where((lane >= 4) & (lane < 13), moved, 0.0)
    ring = pltpu.roll(own, HALF - 8, 1, stride=1, stride_axis=0)
    edge = iota((8, HALF), 1)
    none = jnp.zeros((8, HALF), f32)
    near = ring[HALF - 8:HALF]
    far = ring[HALF:HALF + 8]
    left = jnp.concatenate([ring[HALF - 16:HALF - 8], jnp.where(edge < 8, 0.0, near), jnp.where(edge >= HALF - 8, far, 0.0), none], axis=0)
    right = jnp.concatenate([none, jnp.where(edge < 8, near, 0.0), jnp.where(edge >= HALF - 8, 0.0, far), ring[HALF + 8:HALF + 16]], axis=0)
    zero = jnp.zeros((HALF - 16, HALF), bf16)
    left = jnp.concatenate([ring[:HALF - 16].astype(bf16), left.astype(bf16), zero], axis=0)
    right = jnp.concatenate([zero, right.astype(bf16), ring[HALF + 16:].astype(bf16)], axis=0)
    return jnp.concatenate([left, right], axis=1)


def lane_valid(rows):
    lane = iota((rows, LANES), 1)
    col = iota((rows, LANES), 0) + lane % WIN - RADIUS
    return (col >= 0) & (col < rows) & (lane < K)


def corr_rows(turned_ref, second_ref, start, before, put):
    rows, cols = turned_ref.shape[0], turned_ref.shape[1]
    count = second_ref.shape[0]
    lane = iota((cols, LANES), 1)
    valid = lane_valid(cols)
    mirror = mirror_of(cols)
    for r in range(rows):
        dys = [q - r + RADIUS for q in range(start, start + count) if abs(q - r) <= RADIUS]
        if not dys:
            put(r, before[r])
            continue
        acc = jnp.zeros((cols, LANES), f32)
        for dyi in dys:
            band = band_of(dot(turned_ref[r], second_ref[r + dyi - RADIUS - start], NT), dyi)
            acc = jnp.where((lane >= 9 * dyi) & (lane < 9 * dyi + 9), band, acc)
        acc = jnp.where(valid, dot(mirror, (acc * (C ** -0.5)).astype(bf16)), 0.0)
        if before is None:
            acc = jnp.where(lane == K, 1.0, acc)
        else:
            inside = (lane >= 9 * dys[0]) & (lane < 9 * dys[-1] + 9)
            acc = jnp.where(inside, acc, before[r].astype(f32))
        put(r, acc.astype(bf16))


def mirror_of(cols):
    return (iota((cols, cols), 0) + iota((cols, cols), 1) == cols - 1).astype(bf16)


def by_side(below, body):
    pl.when(below)(lambda: body(True))
    pl.when(jnp.logical_not(below))(lambda: body(False))


def corr_near_body(index_ref, first_ref, own_ref, inner_ref, corr_ref, turned_ref, mid_ref):
    rows, cols = first_ref.shape[0], first_ref.shape[1]
    mirror = mirror_of(cols)
    for r in range(rows):
        turned_ref[r] = dot(mirror, first_ref[r]).astype(bf16)
    corr_rows(turned_ref, own_ref, 0, None, lambda r, v: mid_ref.__setitem__(r, v))

    def side(below):
        corr_rows(turned_ref, inner_ref, rows if below else -rows, mid_ref, lambda r, v: corr_ref.__setitem__(r, v))

    by_side(index_ref[0] & 1 == 0, side)


def corr_outer_body(index_ref, turned_ref, old_ref, outer_ref, corr_ref, ea_ref, eb_ref):
    rows = turned_ref.shape[0]
    par = index_ref[0] & 1

    def side(below):
        corr_rows(turned_ref, outer_ref, rows if below else -rows, old_ref, lambda r, v: corr_ref.__setitem__(r, v))
        ea_ref[...] = corr_ref[0 if below else rows - 1]
        eb_ref[...] = corr_ref[rows - 1 if below else 0]

    by_side(par == 1, side)


def shift_down(x, steps):
    zero = jnp.zeros((abs(steps), x.shape[1]), x.dtype)
    if steps > 0:
        return jnp.concatenate([zero, x[:-steps]], axis=0)
    return jnp.concatenate([x[-steps:], zero], axis=0)


def put_taps(x_ref, slot, value):
    wide = value.astype(f32)
    x_ref[slot, :, 0:LANES] = shift_down(wide, 1).astype(bf16)
    x_ref[slot, :, LANES:2 * LANES] = value
    x_ref[slot, :, 2 * LANES:] = shift_down(wide, -1).astype(bf16)


def cell_row(pre, r, head, target_ref, mask_ref):
    cols = pre.shape[0]
    sig = lax.logistic(pre)
    hidden = (pre * sig).astype(bf16)
    pred = dot(head, hidden, NT)
    err = mask_ref[r:r + 1, :] * (pred[0:2] - target_ref[:, r, :])
    err = jnp.concatenate([err, jnp.zeros((head.shape[0] - 2, cols), f32)], axis=0).astype(bf16)
    herr = dot(err, head, TN)
    pe = (herr * sig * (1.0 + pre * (1.0 - sig))).astype(bf16)
    return pe, dot(err, hidden)


def conv_own_body(corr_ref, w_ref, bias_ref, head_ref, target_ref, mask_ref, x_ref, pre_ref, pe_ref, part_ref, hsum_ref, pt_ref):
    rows, cols = corr_ref.shape[0], corr_ref.shape[1]
    for r in range(rows):
        put_taps(x_ref, r, corr_ref[r])
    head = head_ref[...]
    pre_ref[0] = bias_ref[...] + (dot(x_ref[0], w_ref[1]) + dot(x_ref[1], w_ref[2]))
    pre_ref[1] = bias_ref[...] + (dot(x_ref[rows - 2], w_ref[0]) + dot(x_ref[rows - 1], w_ref[1]))
    total = jnp.zeros(hsum_ref.shape, f32)
    for r in range(1, rows - 1):
        pre = bias_ref[...] + (dot(x_ref[r - 1], w_ref[0]) + dot(x_ref[r], w_ref[1]) + dot(x_ref[r + 1], w_ref[2]))
        pe, head_sum = cell_row(pre, r, head, target_ref, mask_ref)
        total = total + head_sum
        pe_ref[r - 1] = pe
        pt_ref[:, (r - 1) * cols:r * cols] = pe.T
    hsum_ref[...] = total
    for ty in range(3):
        x = x_ref[ty:ty + rows - 2].reshape((rows - 2) * cols, 3 * LANES)
        part_ref[:, ty * 3 * LANES:(ty + 1) * 3 * LANES] = dot(pt_ref[...], x)


def conv_edge_body(par_ref, x_ref, pre_ref, part_ref, hsum_ref, ha_ref, hb_ref, w_ref, head_ref, target_ref, mask_ref,
                   pe_ref, pa_ref, pb_ref, keep_ref, send_ref, h_ref, pt_ref):
    rows, cols = x_ref.shape[0], x_ref.shape[1]
    hid = w_ref.shape[2]
    par = par_ref[0] & 1
    put_taps(h_ref, 1 - par, ha_ref[...])
    put_taps(h_ref, par, hb_ref[...])
    head = head_ref[...]
    head_sum = hsum_ref[...]
    for i, r in enumerate((0, rows - 1)):
        pre = pre_ref[i] + dot(h_ref[i], w_ref[2 * i])
        pe, own_sum = cell_row(pre, r, head, target_ref, mask_ref)
        head_sum = head_sum + own_sum
        pe_ref[i] = pe
        pt_ref[i] = pe.T
    pa_ref[...] = pe_ref[1 - par]
    pb_ref[...] = pe_ref[par]
    top, bottom = pt_ref[0], pt_ref[1]
    pieces = []
    bias_col = None
    for ty in range(3):
        low = h_ref[0] if ty == 0 else x_ref[ty - 1]
        high = h_ref[1] if ty == 2 else x_ref[rows - 2 + ty]
        part = part_ref[:, ty * 3 * LANES:(ty + 1) * 3 * LANES] + (dot(top, low) + dot(bottom, high))
        for tx in range(3):
            pieces.append(part[:, tx * LANES:tx * LANES + K])
        if ty == 1:
            bias_col = part[:, LANES + K:LANES + K + 1]
    head_cols = jnp.concatenate([head_sum, jnp.zeros((LANES - head.shape[0], hid), f32)], axis=0).T
    pad = jnp.zeros((hid, WIDTH - 9 * K - 3), f32)
    sums = jnp.concatenate(pieces + [bias_col, head_cols[:, 0:2], pad], axis=1)
    upper, lower = sums[:hid // 2], sums[hid // 2:]
    keep_ref[...] = jnp.where(par == 0, upper, lower)
    send_ref[...] = jnp.where(par == 0, lower, upper)


def halve_body(index_ref, own_ref, got_ref, keep_ref, send_ref, *, step):
    half = keep_ref.shape[0]
    bit = (index_ref[0] >> step) & 1
    upper = own_ref[:half] + got_ref[:half].astype(f32)
    lower = own_ref[half:] + got_ref[half:].astype(f32)
    keep_ref[...] = jnp.where(bit == 0, upper, lower)
    send_ref[...] = jnp.where(bit == 0, lower, upper).astype(send_ref.dtype)


def piece_body(own_ref, got_ref, piece_ref, send_ref):
    piece = own_ref[...] + got_ref[...].astype(f32)
    piece_ref[...] = piece
    send_ref[...] = piece.astype(bf16)


def add_body(own_ref, got_ref, out_ref):
    out_ref[...] = own_ref[...] + got_ref[...]


def tail_body(index_ref, own_ref, got_ref, conv_ref, rest_ref, square_ref, *, step):
    both = own_ref[...] + got_ref[...].astype(f32)
    share = conv_ref.shape[1]
    piece = jnp.where((index_ref[0] >> step) & 1 == 0, both[:share], both[share:])
    for tap in range(9):
        conv_ref[tap] = piece[:, tap * K:(tap + 1) * K]
    start = 9 * K // LANES * LANES
    rest = jnp.concatenate([piece[:, start:start + LANES], jnp.zeros((LANES - share, LANES), f32)], axis=0)
    rest_ref[...] = rest.T[9 * K - start:9 * K - start + 3, 0:share]
    square_ref[...] = jnp.broadcast_to(jnp.sum(both * both).reshape(1, 1), square_ref.shape)


def final_body(sq_ref, got_ref, conv_ref, rest_ref, out_ref, bias_ref, head_ref, *, limit):
    factor = jnp.minimum(1.0, limit / jnp.sqrt(sq_ref[0:1, 0:1] + got_ref[0:1, 0:1] + 1e-06))
    out_ref[...] = conv_ref[...] * factor.reshape(1, 1, 1)
    bias_ref[...] = rest_ref[0:1] * factor
    head_ref[...] = rest_ref[1:3] * factor


def cerr_row(z0, z1, z2):
    z = z0 + z1 + z2
    return shift_down(z[:, 0:LANES], -1) + z[:, LANES:2 * LANES] + shift_down(z[:, 2 * LANES:], 1)


def cerr_own_body(mid_ref, edge_ref, w_ref, ce_ref, rest_ref):
    rows = mid_ref.shape[0] + 2
    cols = mid_ref.shape[1]
    valid = lane_valid(cols)
    row = lambda r: edge_ref[0] if r == 0 else (edge_ref[1] if r == rows - 1 else mid_ref[r - 1])
    for r in range(rows):
        parts = [dot(row(r + 1 - ty), w_ref[ty], NT) for ty in range(3) if 0 <= r + 1 - ty < rows]
        total = cerr_row(parts[0], parts[1], parts[2] if len(parts) == 3 else 0.0)
        if 0 < r < rows - 1:
            ce_ref[r - 1] = jnp.where(valid, total * (C ** -0.5), 0.0).astype(bf16)
        else:
            rest_ref[min(r, 1)] = total


def cerr_edge_body(par_ref, mid_ref, rest_ref, ha_ref, hb_ref, w_ref, ce_ref, ea_ref, eb_ref, h_ref):
    rows = mid_ref.shape[0] + 2
    cols = mid_ref.shape[1]
    par = par_ref[0] & 1
    h_ref[1 - par] = ha_ref[...]
    h_ref[par] = hb_ref[...]
    valid = lane_valid(cols)
    lane = iota((cols, LANES), 1)
    for i in range(2):
        total = rest_ref[i] + cerr_row(dot(h_ref[i], w_ref[2 - 2 * i], NT), 0.0, 0.0)
        ce_ref[i] = jnp.where(valid, total * (C ** -0.5), 0.0).astype(bf16)
    to_low = jnp.zeros((cols, LANES), f32)
    to_high = jnp.zeros((cols, LANES), f32)
    low_at = high_at = 0
    for r in range(rows):
        total = (ce_ref[min(r, 1)] if r in (0, rows - 1) else mid_ref[r - 1]).astype(f32)
        count = 9 * (RADIUS - r)
        moved = pltpu.roll(total, low_at, 1) if low_at else total
        to_low = jnp.where((lane >= low_at) & (lane < low_at + count), moved, to_low)
        low_at += count
        count = 9 * (r + 1 + RADIUS - rows)
        start = K - count
        moved = pltpu.roll(total, (high_at - start) % LANES, 1)
        to_high = jnp.where((lane >= high_at) & (lane < high_at + count), moved, to_high)
        high_at += count
    up = to_low.astype(bf16)
    down = to_high.astype(bf16)

    @pl.when(par == 0)
    def _():
        ea_ref[...] = down
        eb_ref[...] = up

    @pl.when(par != 0)
    def _():
        ea_ref[...] = up
        eb_ref[...] = down


def row_grad_body(index_ref, ce_ref, first_ref, second_ref, inner_ref, outer_ref, *refs, r, at, done):
    fg_ref, part_ref = refs[-2:]
    old_ref = refs[0] if len(refs) > 2 else None
    rows, cols = first_ref.shape[0], first_ref.shape[1]
    even = index_ref[0] & 1 == 0
    bands = ce_ref[at].astype(f32)
    turned = first_ref[r].T
    acc = jnp.zeros((cols, C), f32)
    for dyi in range(WIN):
        q = r + dyi - RADIUS
        if q < 0:
            src = jnp.where(even, outer_ref[q + rows], inner_ref[q + rows])
        elif q >= rows:
            src = jnp.where(even, inner_ref[q - rows], outer_ref[q - rows])
        else:
            src = second_ref[q]
        spread = spread_of(bands, dyi)
        acc = acc + dot(spread, src)
        if 0 <= q < rows:
            gave = dot(turned, spread)
            part_ref[q] = gave if old_ref is None else old_ref[q] + gave
    fg_ref[r if done else 0] = acc.astype(bf16)
    for other, row_ref in zip(done, refs[1:]):
        fg_ref[other] = row_ref[0]


def halo_parts(bands_ref, rows_ref, below, old_ref):
    rows = old_ref.shape[0]
    bands = bands_ref[...].astype(f32)
    parts = [old_ref[q] for q in range(rows)]
    slot = 0
    for r in range(rows):
        turned = rows_ref[r].T
        for q in range(rows + r - RADIUS, rows) if below else range(0, r + RADIUS + 1 - rows):
            parts[q] = parts[q] + dot(turned, spread_of(bands, slot))
            slot += 1
    return parts


def halo_inner_body(index_ref, bands_ref, rows_ref, old_ref, part_ref):
    def side(below):
        for q, part in enumerate(halo_parts(bands_ref, rows_ref, below, old_ref)):
            part_ref[q] = part

    by_side(index_ref[0] & 1 == 0, side)


def halo_outer_body(index_ref, bands_ref, rows_ref, old_ref, sg_ref):
    def side(below):
        for q, part in enumerate(halo_parts(bands_ref, rows_ref, below, old_ref)):
            sg_ref[q] = part.T.astype(bf16)

    by_side(index_ref[0] & 1 == 1, side)


def on_device(first_map, second_map, flow_target, valid_tiles, conv_weight, conv_bias, head_weight):
    rows, cols = first_map.shape[0], first_map.shape[1]
    hid = conv_weight.shape[2]
    count = lax.axis_size("region")
    index = lax.axis_index("region")
    par = index.reshape(1)
    inner = [(i, i ^ 1) for i in range(count)]
    outer = [(i, i + 1) for i in range(1, count - 1, 2)]
    outer = outer + [(b, a) for a, b in outer]

    def permute(x, pairs):
        return lax.ppermute(x, "region", pairs)

    def swap(x, step):
        return permute(x, [(i, i ^ (1 << step)) for i in range(count)])

    second_outer = permute(second_map, outer)
    second_inner = permute(second_map, inner)
    first_inner = permute(first_map, inner)

    share = hid // count
    radix = [2] * (count.bit_length() - 1)
    turn = tuple(reversed(range(len(radix)))) + (len(radix),)

    def reorder(x):
        return jnp.transpose(x.reshape(tuple(radix) + (share,)), turn).reshape(hid)

    order = reorder(jnp.arange(hid))
    select = (jnp.arange(hid)[:, None] == order[None, :]).astype(bf16)
    weight = jnp.einsum("tkh,hg->tkg", conv_weight, select, preferred_element_type=bf16)
    weight = jnp.pad(weight, ((0, 0), (0, LANES - K), (0, 0))).reshape(3, 3 * LANES, hid)
    head = jnp.einsum("jh,hg->jg", head_weight, select, preferred_element_type=bf16)
    head = jnp.pad(head, ((0, 14), (0, 0)))
    bias = reorder(conv_bias).reshape(1, hid)
    tile_rows = jnp.repeat(valid_tiles, TILE, axis=0)
    own_tiles = lax.dynamic_slice_in_dim(tile_rows, index * rows, rows, 0)
    mask = jnp.repeat(own_tiles, TILE, axis=1).astype(f32)

    vector = lambda *s: pltpu.VMEM(s, bf16)
    corr_near, turned = call(
        corr_near_body,
        [((rows, cols, LANES), bf16), ((rows, cols, C), bf16)],
        (par, first_map, second_map, second_inner),
        scratch=[vector(rows, cols, LANES)],
        scalar=True,
    )
    weight, head, bias, mask, corr_near, second_outer, first_inner = lax.optimization_barrier(
        (weight, head, bias, mask, corr_near, second_outer, first_inner)
    )
    corr, edge_a, edge_b = call(
        corr_outer_body,
        [((rows, cols, LANES), bf16), ((cols, LANES), bf16), ((cols, LANES), bf16)],
        (par, turned, corr_near, second_outer),
        scalar=True,
    )
    halo_b = permute(edge_b, outer)
    halo_a = permute(edge_a, inner)
    taps, pre_edge, pe_mid, part_sums, head_part = call(
        conv_own_body,
        [((rows, cols, 3 * LANES), bf16), ((2, cols, hid), f32), ((rows - 2, cols, hid), bf16), ((hid, 9 * LANES), f32), ((16, hid), f32)],
        (corr, weight, bias, head, flow_target, mask),
        scratch=[vector(hid, (rows - 2) * cols)],
    )
    halo_a, halo_b, taps = lax.optimization_barrier((halo_a, halo_b, taps))
    pe_edge, pe_a, pe_b, keep, send = call(
        conv_edge_body,
        [((2, cols, hid), bf16), ((cols, hid), bf16), ((cols, hid), bf16), ((hid // 2, WIDTH), f32), ((hid // 2, WIDTH), f32)],
        (par, taps, pre_edge, part_sums, head_part, halo_a, halo_b, weight, head, flow_target, mask),
        scratch=[vector(2, cols, 3 * LANES), vector(2, hid, cols)],
        scalar=True,
    )
    got = swap(send, 0)
    pe_halo_a = permute(pe_a, inner)
    pe_halo_b = permute(pe_b, outer)

    def add(x, y):
        return call(add_body, [(x.shape, f32)], (x, y))[0]

    def halve(step, keep, got):
        half = keep.shape[0] // 2
        return call(functools.partial(halve_body, step=step), [((half, WIDTH), f32), ((half, WIDTH), bf16)], (par, keep, got), scalar=True)

    def row_grad(r, at, cerr, part, done=()):
        args = (par, cerr, first_map, second_map, second_inner, second_outer)
        if part is not None:
            args = args + (part,) + tuple(row for _, row in done)
        return call(
            functools.partial(row_grad_body, r=r, at=at, done=[other for other, _ in done]),
            [((rows if done else 1, cols, C), bf16), ((rows, C, cols), f32)],
            args,
            scalar=True,
            alias=None if part is None else {6: 1},
        )

    steps = len(radix)
    keep, send = halve(1, keep, got)
    got = swap(send, 1)
    ce_mid, ce_rest = call(
        cerr_own_body,
        [((rows - 2, cols, LANES), bf16), ((2, cols, LANES), f32)],
        (after(pe_mid, send), pe_edge, weight),
    )
    part = None
    done = []
    for r in range(1, rows - 1):
        row, part = row_grad(r, r - 1, ce_mid, part)
        done.append((r, row))
    got, part = lax.optimization_barrier((got, part))
    keep, send = halve(2, keep, got)
    got = swap(send, 2)
    ce_edge, ce_a, ce_b = call(
        cerr_edge_body,
        [((2, cols, LANES), bf16), ((cols, LANES), bf16), ((cols, LANES), bf16)],
        (par, ce_mid, after(ce_rest, send), pe_halo_a, pe_halo_b, weight),
        scratch=[vector(2, cols, hid)],
        scalar=True,
    )
    ce_outer = permute(ce_b, outer)
    ce_inner = permute(ce_a, inner)
    first_outer = permute(after(first_map, ce_a), outer)
    got, ce_edge, part = lax.optimization_barrier((got, ce_edge, part))
    for step in range(3, steps - 1):
        keep, send = halve(step, keep, got)
        got = swap(send, step)
    piece, send = call(piece_body, [(keep.shape, f32), (keep.shape, bf16)], (keep, got))
    got = swap(send, steps - 1)
    ce_edge = after(ce_edge, piece)
    row, part = row_grad(0, 0, ce_edge, part)
    done.append((0, row))
    first_grad, part = row_grad(rows - 1, 1, ce_edge, part, done)
    got, part, ce_inner, ce_outer = lax.optimization_barrier((got, part, ce_inner, ce_outer))
    conv_raw, rest_raw, square = call(
        functools.partial(tail_body, step=steps - 1),
        [((9, share, K), f32), ((3, share), f32), ((8, LANES), f32)],
        (par, piece, got),
        scalar=True,
    )
    got = swap(square, 0)
    square = add(square, got)
    got = swap(square, 1)
    (part,) = call(
        halo_inner_body,
        [((rows, C, cols), f32)],
        (par, after(ce_inner, square), first_inner, part),
        scalar=True,
        alias={3: 0},
    )
    got, part = lax.optimization_barrier((got, part))
    square = add(square, got)
    got = swap(square, 2)
    (second_grad,) = call(
        halo_outer_body,
        [((rows, cols, C), bf16)],
        (par, after(ce_outer, square), first_outer, part),
        scalar=True,
    )
    got, second_grad = lax.optimization_barrier((got, second_grad))
    for step in range(3, steps - 1):
        square = add(square, got)
        got = swap(square, step)
    param_count = 9 * K * hid + 3 * hid
    conv_piece, bias_piece, head_piece = call(
        functools.partial(final_body, limit=clip_fraction * param_count ** 0.5),
        [((9, share, K), f32), ((1, share), f32), ((2, share), f32)],
        (square, got, conv_raw, rest_raw),
    )
    return first_grad, second_grad, jnp.transpose(conv_piece, (0, 2, 1)), bias_piece.reshape(share), head_piece


def solution(mesh):
    return jax.shard_map(
        on_device,
        mesh=mesh,
        in_specs=(
            P("region", "group", None),
            P("region", "group", None),
            P(None, "region", "group"),
            P(None, "group"),
            P(),
            P(),
            P(),
        ),
        out_specs=(
            P("region", "group", None),
            P("region", "group", None),
            P("group", None, "region"),
            P(("group", "region")),
            P("group", "region"),
        ),
        check_vma=False,
    )
```

```python
import functools

import jax
import jax.numpy as jnp
from jax import lax
from jax.experimental import pallas as pl
from jax.experimental.pallas import tpu as pltpu
from jax.sharding import PartitionSpec as P

C = 256
RADIUS = 4
TILE = 16
K = 81
WIN = 9
LANES = 128

clip_fraction = 0.25
WIDTH = 768
VMEM_LIMIT = 24 * 1024 * 1024

f32 = jnp.float32
bf16 = jnp.bfloat16

NT = (((1,), (1,)), ((), ()))
TN = (((0,), (0,)), ((), ()))


def dot(a, b, dims=None):
    if dims is None:
        return jnp.dot(a, b, preferred_element_type=f32)
    return lax.dot_general(a, b, dims, preferred_element_type=f32)


def iota(shape, dim):
    return lax.broadcasted_iota(jnp.int32, shape, dim)


SMEM = pl.BlockSpec(memory_space=pltpu.SMEM)
VMEM = pl.BlockSpec(memory_space=pltpu.VMEM)


def call(body, outs, args, scratch=(), scalar=False, alias=None, first_any=False):
    specs = [VMEM] * len(args)
    if scalar:
        specs[0] = SMEM
    return pl.pallas_call(
        body,
        out_shape=[jax.ShapeDtypeStruct(s, d) for s, d in outs],
        in_specs=specs,
        out_specs=[pl.BlockSpec(memory_space=pl.ANY) if first_any and i == 0 else VMEM for i in range(len(outs))],
        scratch_shapes=list(scratch),
        input_output_aliases=alias or {},
        compiler_params=pltpu.CompilerParams(vmem_limit_bytes=VMEM_LIMIT),
    )(*args)


def after(value, *others):
    return lax.optimization_barrier((value,) + others)[0]


HALF = LANES


def band_of(products, dyi):
    lane = iota((8, HALF), 1)
    near = jnp.where(lane >= HALF - 8, products[HALF - 8:HALF, :HALF], products[HALF - 8:HALF, HALF:])
    far = jnp.where(lane < 8, products[HALF:HALF + 8, HALF:], products[HALF:HALF + 8, :HALF])
    ring = jnp.concatenate([products[:HALF - 8, HALF:], near, far, products[HALF + 8:, :HALF]], axis=0)
    band = pltpu.roll(ring, 8, 1, stride=1, stride_axis=0)
    return pltpu.roll(band, (9 * dyi - 3) % LANES, 1)


def spread_of(bands, dyi):
    moved = pltpu.roll(bands, (4 - 9 * dyi) % LANES, 1)
    lane = iota(bands.shape, 1)
    own = jnp.where((lane >= 4) & (lane < 13), moved, 0.0)
    ring = pltpu.roll(own, HALF - 8, 1, stride=1, stride_axis=0)
    edge = iota((8, HALF), 1)
    none = jnp.zeros((8, HALF), f32)
    near = ring[HALF - 8:HALF]
    far = ring[HALF:HALF + 8]
    left = jnp.concatenate([ring[HALF - 16:HALF - 8], jnp.where(edge < 8, 0.0, near), jnp.where(edge >= HALF - 8, far, 0.0), none], axis=0)
    right = jnp.concatenate([none, jnp.where(edge < 8, near, 0.0), jnp.where(edge >= HALF - 8, 0.0, far), ring[HALF + 8:HALF + 16]], axis=0)
    zero = jnp.zeros((HALF - 16, HALF), bf16)
    left = jnp.concatenate([ring[:HALF - 16].astype(bf16), left.astype(bf16), zero], axis=0)
    right = jnp.concatenate([zero, right.astype(bf16), ring[HALF + 16:].astype(bf16)], axis=0)
    return jnp.concatenate([left, right], axis=1)


def lane_valid(rows):
    lane = iota((rows, LANES), 1)
    col = iota((rows, LANES), 0) + lane % WIN - RADIUS
    return (col >= 0) & (col < rows) & (lane < K)


def corr_rows(turned_ref, second_ref, start, before, put):
    rows, cols = turned_ref.shape[0], turned_ref.shape[1]
    count = second_ref.shape[0]
    lane = iota((cols, LANES), 1)
    valid = lane_valid(cols)
    mirror = mirror_of(cols)
    for r in range(rows):
        dys = [q - r + RADIUS for q in range(start, start + count) if abs(q - r) <= RADIUS]
        if not dys:
            put(r, before[r])
            continue
        acc = jnp.zeros((cols, LANES), f32)
        for dyi in dys:
            band = band_of(dot(turned_ref[r], second_ref[r + dyi - RADIUS - start], NT), dyi)
            acc = jnp.where((lane >= 9 * dyi) & (lane < 9 * dyi + 9), band, acc)
        acc = jnp.where(valid, dot(mirror, (acc * (C ** -0.5)).astype(bf16)), 0.0)
        if before is None:
            acc = jnp.where(lane == K, 1.0, acc)
        else:
            inside = (lane >= 9 * dys[0]) & (lane < 9 * dys[-1] + 9)
            acc = jnp.where(inside, acc, before[r].astype(f32))
        put(r, acc.astype(bf16))


def mirror_of(cols):
    return (iota((cols, cols), 0) + iota((cols, cols), 1) == cols - 1).astype(bf16)


def by_side(below, body):
    pl.when(below)(lambda: body(True))
    pl.when(jnp.logical_not(below))(lambda: body(False))


def corr_near_body(index_ref, first_ref, own_ref, inner_ref, corr_ref, turned_ref, mid_ref):
    rows, cols = first_ref.shape[0], first_ref.shape[1]
    mirror = mirror_of(cols)
    for r in range(rows):
        turned_ref[r] = dot(mirror, first_ref[r]).astype(bf16)
    corr_rows(turned_ref, own_ref, 0, None, lambda r, v: mid_ref.__setitem__(r, v))

    def side(below):
        corr_rows(turned_ref, inner_ref, rows if below else -rows, mid_ref, lambda r, v: corr_ref.__setitem__(r, v))

    by_side(index_ref[0] & 1 == 0, side)


def corr_outer_body(index_ref, turned_ref, old_ref, outer_ref, corr_ref, ea_ref, eb_ref):
    rows = turned_ref.shape[0]
    par = index_ref[0] & 1

    def side(below):
        corr_rows(turned_ref, outer_ref, rows if below else -rows, old_ref, lambda r, v: corr_ref.__setitem__(r, v))
        ea_ref[...] = corr_ref[0 if below else rows - 1]
        eb_ref[...] = corr_ref[rows - 1 if below else 0]

    by_side(par == 1, side)


def shift_down(x, steps):
    zero = jnp.zeros((abs(steps), x.shape[1]), x.dtype)
    if steps > 0:
        return jnp.concatenate([zero, x[:-steps]], axis=0)
    return jnp.concatenate([x[-steps:], zero], axis=0)


def put_taps(x_ref, slot, value):
    wide = value.astype(f32)
    x_ref[slot, :, 0:LANES] = shift_down(wide, 1).astype(bf16)
    x_ref[slot, :, LANES:2 * LANES] = value
    x_ref[slot, :, 2 * LANES:] = shift_down(wide, -1).astype(bf16)


def cell_row(pre, r, head, target_ref, mask_ref):
    cols = pre.shape[0]
    sig = lax.logistic(pre)
    hidden = (pre * sig).astype(bf16)
    pred = dot(head, hidden, NT)
    err = mask_ref[r:r + 1, :] * (pred[0:2] - target_ref[:, r, :])
    err = jnp.concatenate([err, jnp.zeros((head.shape[0] - 2, cols), f32)], axis=0).astype(bf16)
    herr = dot(err, head, TN)
    pe = (herr * sig * (1.0 + pre * (1.0 - sig))).astype(bf16)
    return pe, dot(err, hidden)


def conv_own_body(corr_ref, w_ref, bias_ref, head_ref, target_ref, mask_ref, x_ref, pre_ref, pe_ref, part_ref, hsum_ref, pt_ref):
    rows, cols = corr_ref.shape[0], corr_ref.shape[1]
    for r in range(rows):
        put_taps(x_ref, r, corr_ref[r])
    head = head_ref[...]
    pre_ref[0] = bias_ref[...] + (dot(x_ref[0], w_ref[1]) + dot(x_ref[1], w_ref[2]))
    pre_ref[1] = bias_ref[...] + (dot(x_ref[rows - 2], w_ref[0]) + dot(x_ref[rows - 1], w_ref[1]))
    total = jnp.zeros(hsum_ref.shape, f32)
    for r in range(1, rows - 1):
        pre = bias_ref[...] + (dot(x_ref[r - 1], w_ref[0]) + dot(x_ref[r], w_ref[1]) + dot(x_ref[r + 1], w_ref[2]))
        pe, head_sum = cell_row(pre, r, head, target_ref, mask_ref)
        total = total + head_sum
        pe_ref[r - 1] = pe
        pt_ref[:, (r - 1) * cols:r * cols] = pe.T
    hsum_ref[...] = total
    for ty in range(3):
        x = x_ref[ty:ty + rows - 2].reshape((rows - 2) * cols, 3 * LANES)
        part_ref[:, ty * 3 * LANES:(ty + 1) * 3 * LANES] = dot(pt_ref[...], x)


def conv_edge_body(par_ref, x_ref, pre_ref, part_ref, hsum_ref, ha_ref, hb_ref, w_ref, head_ref, target_ref, mask_ref,
                   pe_ref, pa_ref, pb_ref, keep_ref, send_ref, h_ref, pt_ref):
    rows, cols = x_ref.shape[0], x_ref.shape[1]
    hid = w_ref.shape[2]
    par = par_ref[0] & 1
    put_taps(h_ref, 1 - par, ha_ref[...])
    put_taps(h_ref, par, hb_ref[...])
    head = head_ref[...]
    head_sum = hsum_ref[...]
    for i, r in enumerate((0, rows - 1)):
        pre = pre_ref[i] + dot(h_ref[i], w_ref[2 * i])
        pe, own_sum = cell_row(pre, r, head, target_ref, mask_ref)
        head_sum = head_sum + own_sum
        pe_ref[i] = pe
        pt_ref[i] = pe.T
    pa_ref[...] = pe_ref[1 - par]
    pb_ref[...] = pe_ref[par]
    top, bottom = pt_ref[0], pt_ref[1]
    pieces = []
    bias_col = None
    for ty in range(3):
        low = h_ref[0] if ty == 0 else x_ref[ty - 1]
        high = h_ref[1] if ty == 2 else x_ref[rows - 2 + ty]
        part = part_ref[:, ty * 3 * LANES:(ty + 1) * 3 * LANES] + (dot(top, low) + dot(bottom, high))
        for tx in range(3):
            pieces.append(part[:, tx * LANES:tx * LANES + K])
        if ty == 1:
            bias_col = part[:, LANES + K:LANES + K + 1]
    head_cols = jnp.concatenate([head_sum, jnp.zeros((LANES - head.shape[0], hid), f32)], axis=0).T
    pad = jnp.zeros((hid, WIDTH - 9 * K - 3), f32)
    sums = jnp.concatenate(pieces + [bias_col, head_cols[:, 0:2], pad], axis=1)
    upper, lower = sums[:hid // 2], sums[hid // 2:]
    keep_ref[...] = jnp.where(par == 0, upper, lower)
    send_ref[...] = jnp.where(par == 0, lower, upper)


def halve_body(index_ref, own_ref, got_ref, keep_ref, send_ref, *, step):
    half = keep_ref.shape[0]
    bit = (index_ref[0] >> step) & 1
    upper = own_ref[:half] + got_ref[:half].astype(f32)
    lower = own_ref[half:] + got_ref[half:].astype(f32)
    keep_ref[...] = jnp.where(bit == 0, upper, lower)
    send_ref[...] = jnp.where(bit == 0, lower, upper).astype(send_ref.dtype)


def piece_body(own_ref, got_ref, piece_ref, send_ref):
    piece = own_ref[...] + got_ref[...].astype(f32)
    piece_ref[...] = piece
    send_ref[...] = piece.astype(bf16)


def add_body(own_ref, got_ref, out_ref):
    out_ref[...] = own_ref[...] + got_ref[...]


def tail_body(index_ref, own_ref, got_ref, conv_ref, rest_ref, square_ref, *, step):
    both = own_ref[...] + got_ref[...].astype(f32)
    share = conv_ref.shape[1]
    piece = jnp.where((index_ref[0] >> step) & 1 == 0, both[:share], both[share:])
    for tap in range(9):
        conv_ref[tap] = piece[:, tap * K:(tap + 1) * K]
    start = 9 * K // LANES * LANES
    rest = jnp.concatenate([piece[:, start:start + LANES], jnp.zeros((LANES - share, LANES), f32)], axis=0)
    rest_ref[...] = rest.T[9 * K - start:9 * K - start + 3, 0:share]
    square_ref[...] = jnp.broadcast_to(jnp.sum(both * both).reshape(1, 1), square_ref.shape)


def final_body(sq_ref, got_ref, conv_ref, rest_ref, out_ref, bias_ref, head_ref, *, limit):
    factor = jnp.minimum(1.0, limit / jnp.sqrt(sq_ref[0:1, 0:1] + got_ref[0:1, 0:1] + 1e-06))
    out_ref[...] = conv_ref[...] * factor.reshape(1, 1, 1)
    bias_ref[...] = rest_ref[0:1] * factor
    head_ref[...] = rest_ref[1:3] * factor


def cerr_row(z0, z1, z2):
    z = z0 + z1 + z2
    return shift_down(z[:, 0:LANES], -1) + z[:, LANES:2 * LANES] + shift_down(z[:, 2 * LANES:], 1)


def cerr_own_body(mid_ref, edge_ref, w_ref, ce_ref, rest_ref):
    rows = mid_ref.shape[0] + 2
    cols = mid_ref.shape[1]
    valid = lane_valid(cols)
    row = lambda r: edge_ref[0] if r == 0 else (edge_ref[1] if r == rows - 1 else mid_ref[r - 1])
    for r in range(rows):
        parts = [dot(row(r + 1 - ty), w_ref[ty], NT) for ty in range(3) if 0 <= r + 1 - ty < rows]
        total = cerr_row(parts[0], parts[1], parts[2] if len(parts) == 3 else 0.0)
        if 0 < r < rows - 1:
            ce_ref[r - 1] = jnp.where(valid, total * (C ** -0.5), 0.0).astype(bf16)
        else:
            rest_ref[min(r, 1)] = total


def cerr_edge_body(par_ref, mid_ref, rest_ref, ha_ref, hb_ref, w_ref, ce_ref, ea_ref, eb_ref, h_ref):
    rows = mid_ref.shape[0] + 2
    cols = mid_ref.shape[1]
    par = par_ref[0] & 1
    h_ref[1 - par] = ha_ref[...]
    h_ref[par] = hb_ref[...]
    valid = lane_valid(cols)
    lane = iota((cols, LANES), 1)
    for i in range(2):
        total = rest_ref[i] + cerr_row(dot(h_ref[i], w_ref[2 - 2 * i], NT), 0.0, 0.0)
        ce_ref[i] = jnp.where(valid, total * (C ** -0.5), 0.0).astype(bf16)
    to_low = jnp.zeros((cols, LANES), f32)
    to_high = jnp.zeros((cols, LANES), f32)
    low_at = high_at = 0
    for r in range(rows):
        total = (ce_ref[min(r, 1)] if r in (0, rows - 1) else mid_ref[r - 1]).astype(f32)
        count = 9 * (RADIUS - r)
        moved = pltpu.roll(total, low_at, 1) if low_at else total
        to_low = jnp.where((lane >= low_at) & (lane < low_at + count), moved, to_low)
        low_at += count
        count = 9 * (r + 1 + RADIUS - rows)
        start = K - count
        moved = pltpu.roll(total, (high_at - start) % LANES, 1)
        to_high = jnp.where((lane >= high_at) & (lane < high_at + count), moved, to_high)
        high_at += count
    up = to_low.astype(bf16)
    down = to_high.astype(bf16)

    @pl.when(par == 0)
    def _():
        ea_ref[...] = down
        eb_ref[...] = up

    @pl.when(par != 0)
    def _():
        ea_ref[...] = up
        eb_ref[...] = down


def row_grad_body(index_ref, ce_ref, first_ref, second_ref, inner_ref, outer_ref, *refs, r, at, done):
    copies = []
    if done:
        *refs, own_ref, sems = refs
        copies = [
            pltpu.make_async_copy(row_ref.at[0], refs[-2].at[other], sems.at[i])
            for i, (other, row_ref) in enumerate(zip(done, refs[1:]))
        ]
        for copy in copies:
            copy.start()
    fg_ref, part_ref = refs[-2:]
    old_ref = refs[0] if len(refs) > 2 else None
    rows, cols = first_ref.shape[0], first_ref.shape[1]
    even = index_ref[0] & 1 == 0
    bands = ce_ref[at].astype(f32)
    turned = first_ref[r].T
    acc = jnp.zeros((cols, C), f32)
    for dyi in range(WIN):
        q = r + dyi - RADIUS
        if q < 0:
            src = jnp.where(even, outer_ref[q + rows], inner_ref[q + rows])
        elif q >= rows:
            src = jnp.where(even, inner_ref[q - rows], outer_ref[q - rows])
        else:
            src = second_ref[q]
        spread = spread_of(bands, dyi)
        acc = acc + dot(spread, src)
        if 0 <= q < rows:
            gave = dot(turned, spread)
            part_ref[q] = gave if old_ref is None else old_ref[q] + gave
    if not done:
        fg_ref[0] = acc.astype(bf16)
        return
    own_ref[...] = acc.astype(bf16)
    copies.append(pltpu.make_async_copy(own_ref, fg_ref.at[r], sems.at[len(done)]))
    copies[-1].start()
    for copy in copies:
        copy.wait()


def halo_parts(bands_ref, rows_ref, below, old_ref):
    rows = old_ref.shape[0]
    bands = bands_ref[...].astype(f32)
    parts = [old_ref[q] for q in range(rows)]
    slot = 0
    for r in range(rows):
        turned = rows_ref[r].T
        for q in range(rows + r - RADIUS, rows) if below else range(0, r + RADIUS + 1 - rows):
            parts[q] = parts[q] + dot(turned, spread_of(bands, slot))
            slot += 1
    return parts


def halo_inner_body(index_ref, bands_ref, rows_ref, old_ref, part_ref):
    def side(below):
        for q, part in enumerate(halo_parts(bands_ref, rows_ref, below, old_ref)):
            part_ref[q] = part

    by_side(index_ref[0] & 1 == 0, side)


def halo_outer_body(index_ref, bands_ref, rows_ref, old_ref, sg_ref, out_ref, sems):
    rows = old_ref.shape[0]
    bands = bands_ref[...].astype(f32)

    def side(below):
        parts = [old_ref[q] for q in range(rows)]
        copies = []
        for r in range(rows) if below else reversed(range(rows)):
            turned = rows_ref[r].T
            if below:
                slot = sum(RADIUS - i for i in range(r))
                ends = range(rows + r - RADIUS, rows)
            else:
                slot = sum(i + RADIUS + 1 - rows for i in range(r))
                ends = range(0, r + RADIUS + 1 - rows)
            for i, q in enumerate(ends):
                parts[q] = parts[q] + dot(turned, spread_of(bands, slot + i))
            out_ref[r] = parts[r].T.astype(bf16)
            copies.append(pltpu.make_async_copy(out_ref.at[r], sg_ref.at[r], sems.at[r]))
            copies[-1].start()
        for copy in copies:
            copy.wait()

    by_side(index_ref[0] & 1 == 1, side)


def on_device(first_map, second_map, flow_target, valid_tiles, conv_weight, conv_bias, head_weight):
    rows, cols = first_map.shape[0], first_map.shape[1]
    hid = conv_weight.shape[2]
    count = lax.axis_size("region")
    index = lax.axis_index("region")
    par = index.reshape(1)
    inner = [(i, i ^ 1) for i in range(count)]
    outer = [(i, i + 1) for i in range(1, count - 1, 2)]
    outer = outer + [(b, a) for a, b in outer]

    def permute(x, pairs):
        return lax.ppermute(x, "region", pairs)

    def swap(x, step):
        return permute(x, [(i, i ^ (1 << step)) for i in range(count)])

    second_outer = permute(second_map, outer)
    second_inner = permute(second_map, inner)
    first_inner = permute(first_map, inner)

    share = hid // count
    radix = [2] * (count.bit_length() - 1)
    turn = tuple(reversed(range(len(radix)))) + (len(radix),)

    def reorder(x):
        return jnp.transpose(x.reshape(tuple(radix) + (share,)), turn).reshape(hid)

    order = reorder(jnp.arange(hid))
    select = (jnp.arange(hid)[:, None] == order[None, :]).astype(bf16)
    weight = jnp.einsum("tkh,hg->tkg", conv_weight, select, preferred_element_type=bf16)
    weight = jnp.pad(weight, ((0, 0), (0, LANES - K), (0, 0))).reshape(3, 3 * LANES, hid)
    head = jnp.einsum("jh,hg->jg", head_weight, select, preferred_element_type=bf16)
    head = jnp.pad(head, ((0, 14), (0, 0)))
    bias = reorder(conv_bias).reshape(1, hid)
    tile_rows = jnp.repeat(valid_tiles, TILE, axis=0)
    own_tiles = lax.dynamic_slice_in_dim(tile_rows, index * rows, rows, 0)
    mask = jnp.repeat(own_tiles, TILE, axis=1).astype(f32)

    vector = lambda *s: pltpu.VMEM(s, bf16)
    corr_near, turned = call(
        corr_near_body,
        [((rows, cols, LANES), bf16), ((rows, cols, C), bf16)],
        (par, first_map, second_map, second_inner),
        scratch=[vector(rows, cols, LANES)],
        scalar=True,
    )
    weight, head, bias, mask, corr_near, second_outer, first_inner = lax.optimization_barrier(
        (weight, head, bias, mask, corr_near, second_outer, first_inner)
    )
    corr, edge_a, edge_b = call(
        corr_outer_body,
        [((rows, cols, LANES), bf16), ((cols, LANES), bf16), ((cols, LANES), bf16)],
        (par, turned, corr_near, second_outer),
        scalar=True,
    )
    halo_b = permute(edge_b, outer)
    halo_a = permute(edge_a, inner)
    taps, pre_edge, pe_mid, part_sums, head_part = call(
        conv_own_body,
        [((rows, cols, 3 * LANES), bf16), ((2, cols, hid), f32), ((rows - 2, cols, hid), bf16), ((hid, 9 * LANES), f32), ((16, hid), f32)],
        (corr, weight, bias, head, flow_target, mask),
        scratch=[vector(hid, (rows - 2) * cols)],
    )
    halo_a, halo_b, taps = lax.optimization_barrier((halo_a, halo_b, taps))
    pe_edge, pe_a, pe_b, keep, send = call(
        conv_edge_body,
        [((2, cols, hid), bf16), ((cols, hid), bf16), ((cols, hid), bf16), ((hid // 2, WIDTH), f32), ((hid // 2, WIDTH), f32)],
        (par, taps, pre_edge, part_sums, head_part, halo_a, halo_b, weight, head, flow_target, mask),
        scratch=[vector(2, cols, 3 * LANES), vector(2, hid, cols)],
        scalar=True,
    )
    got = swap(send, 0)
    pe_halo_a = permute(pe_a, inner)
    pe_halo_b = permute(pe_b, outer)

    def add(x, y):
        return call(add_body, [(x.shape, f32)], (x, y))[0]

    def halve(step, keep, got):
        half = keep.shape[0] // 2
        return call(functools.partial(halve_body, step=step), [((half, WIDTH), f32), ((half, WIDTH), bf16)], (par, keep, got), scalar=True)

    def row_grad(r, at, cerr, part, done=()):
        args = (par, cerr, first_map, second_map, second_inner, second_outer)
        if part is not None:
            args = args + (part,) + tuple(row for _, row in done)
        return call(
            functools.partial(row_grad_body, r=r, at=at, done=[other for other, _ in done]),
            [((rows if done else 1, cols, C), bf16), ((rows, C, cols), f32)],
            args,
            scratch=[vector(cols, C), pltpu.SemaphoreType.DMA((rows,))] if done else (),
            scalar=True,
            alias=None if part is None else {6: 1},
            first_any=bool(done),
        )

    steps = len(radix)
    keep, send = halve(1, keep, got)
    got = swap(send, 1)
    ce_mid, ce_rest = call(
        cerr_own_body,
        [((rows - 2, cols, LANES), bf16), ((2, cols, LANES), f32)],
        (after(pe_mid, send), pe_edge, weight),
    )
    part = None
    done = []
    for r in range(1, rows - 1):
        row, part = row_grad(r, r - 1, ce_mid, part)
        done.append((r, row))
    got, part = lax.optimization_barrier((got, part))
    keep, send = halve(2, keep, got)
    got = swap(send, 2)
    ce_edge, ce_a, ce_b = call(
        cerr_edge_body,
        [((2, cols, LANES), bf16), ((cols, LANES), bf16), ((cols, LANES), bf16)],
        (par, ce_mid, after(ce_rest, send), pe_halo_a, pe_halo_b, weight),
        scratch=[vector(2, cols, hid)],
        scalar=True,
    )
    ce_outer = permute(ce_b, outer)
    ce_inner = permute(ce_a, inner)
    first_outer = permute(after(first_map, ce_a), outer)
    got, ce_edge, part = lax.optimization_barrier((got, ce_edge, part))
    for step in range(3, steps - 1):
        keep, send = halve(step, keep, got)
        got = swap(send, step)
    piece, send = call(piece_body, [(keep.shape, f32), (keep.shape, bf16)], (keep, got))
    got = swap(send, steps - 1)
    ce_edge = after(ce_edge, piece)
    row, part = row_grad(0, 0, ce_edge, part)
    done.append((0, row))
    got, part = lax.optimization_barrier((got, part))
    conv_raw, rest_raw, square = call(
        functools.partial(tail_body, step=steps - 1),
        [((9, share, K), f32), ((3, share), f32), ((8, LANES), f32)],
        (par, piece, got),
        scalar=True,
    )
    got = swap(square, 0)
    square = add(square, got)
    got = swap(square, 1)
    first_grad, part = row_grad(rows - 1, 1, after(ce_edge, square), part, done)
    (part,) = call(
        halo_inner_body,
        [((rows, C, cols), f32)],
        (par, after(ce_inner, square), first_inner, part),
        scalar=True,
        alias={3: 0},
    )
    got, part = lax.optimization_barrier((got, part))
    square = add(square, got)
    got = swap(square, 2)
    (second_grad,) = call(
        halo_outer_body,
        [((rows, cols, C), bf16)],
        (par, after(ce_outer, square), first_outer, part),
        scratch=[vector(rows, cols, C), pltpu.SemaphoreType.DMA((rows,))],
        scalar=True,
        first_any=True,
    )
    got, second_grad = lax.optimization_barrier((got, second_grad))
    for step in range(3, steps - 1):
        square = add(square, got)
        got = swap(square, step)
    param_count = 9 * K * hid + 3 * hid
    conv_piece, bias_piece, head_piece = call(
        functools.partial(final_body, limit=clip_fraction * param_count ** 0.5),
        [((9, share, K), f32), ((1, share), f32), ((2, share), f32)],
        (square, got, conv_raw, rest_raw),
    )
    return first_grad, second_grad, jnp.transpose(conv_piece, (0, 2, 1)), bias_piece.reshape(share), head_piece


def solution(mesh):
    return jax.shard_map(
        on_device,
        mesh=mesh,
        in_specs=(
            P("region", "group", None),
            P("region", "group", None),
            P(None, "region", "group"),
            P(None, "group"),
            P(),
            P(),
            P(),
        ),
        out_specs=(
            P("region", "group", None),
            P("region", "group", None),
            P("group", None, "region"),
            P(("group", "region")),
            P("group", "region"),
        ),
        check_vma=False,
    )
```
